256 devices in a mesh: pool: 8 (over z), expert: 32 (over x, y, core).
Axes of the slice: x: 4, y: 4, z: 8, core: 2. Of those that a mesh axis runs over, the one named last changes fastest.
Arguments:
- residual: bfloat16 [32, 512, 4096], P('expert', 'pool'), may hold values from -36 to 36
- queries: bfloat16 [32, 512, 4096], P('expert', 'pool'), may hold values from -8 to 8
- fresh_kv: bfloat16 [32, 512, 512], P('expert', 'pool'), may hold values from -16 to 16
- pool_cache: bfloat16 [512, 16, 512], P('pool'), may hold values from -16 to 16
- hit_blocks: int32 [32, 16], P('expert'), may hold values from 0 to 511, as said below
- norm_gain: float32 [4096], replicated, may hold values from 0.1 to 1.9
- route_ids: int32 [32, 512, 8], P('expert', 'pool'), may hold values from 0 to 127, all different within a row; in each aligned block of 64 rows (0 to 63, 64 to 127, ..., all dimensions but the last counted through in order) at most 5 rows name the same one
- route_logits: float32 [32, 512, 8], P('expert', 'pool'), may hold values from -310 to 310
- w_gate: bfloat16 [256, 4096, 384], P(('pool', 'expert')), may hold values from -0.25 to 0.25
- w_up: bfloat16 [256, 4096, 384], P(('pool', 'expert')), may hold values from -0.25 to 0.25
- w_down: bfloat16 [256, 384, 4096], P(('pool', 'expert')), may hold values from -0.625 to 0.625
Outputs:
- attended: bfloat16 [32, 512, 4096], P('expert', 'pool')
- layer_out: bfloat16 [32, 512, 4096], P('expert', 'pool')
The draws below stay inside these ranges and needn't reach their ends.
Inputs may be any that keep to these rules, and one draw needn't show every extreme that they name: `hit_blocks`: each request's 16 block ids are distinct; block b is held by pool index b // 64; one pool index holds exactly 4 of a request's blocks, and the others share the rest as evenly as they can. `route_ids`: among the 64 tokens of one device, each expert is chosen by at most 5 of them; some expert is chosen by exactly 5 of some device's tokens.
All inputs are finite; a program needn't handle non-finite values.
Results may differ from the reference program's by a relative error of at most 0.017.
Values may be sent and summed in bfloat16 or wider, within the bound.
No kernel may reach another device: no remote copies, remote signals or barrier semaphores. Data moves between devices by JAX's collectives and lax.ppermute only.
A program may use at most 192 MiB of HBM per device.

```python
import math
import jax
import jax.numpy as jnp
import numpy as np
from jax import lax

D = 4096
HEADS = 32
HD = 128
KVH = 2
FFH = 768
TOPK = 8
TOK_DEV = 64
BLOCK = 16
HITS = 16
PB_DEV = 64
HALF = 384
HOT = 4
EXPERTS = 128
SLABS = 256
MOST = 5
REQUESTS = 32
REQ_LEN = 512
POOL_BLOCKS = 512
N_POOL = 8
DEVICES = 256


def key_value_rows(key, lead, salt):
    part_shape = lead + (KVH, HD)
    key_part = jnp.clip(jax.random.normal(jax.random.fold_in(key, salt), part_shape, jnp.float32), -6.0, 6.0)
    value_part = jnp.clip(4.0 * jax.random.normal(jax.random.fold_in(key, salt + 1), part_shape, jnp.float32), -16.0, 16.0)
    return (key_part, value_part)


def draw_residual(key, part):
    row_scale = jnp.exp(jax.random.uniform(jax.random.fold_in(key, 41), (REQUESTS, REQ_LEN, 1), jnp.float32, -1.15, 1.15))
    col_scale = jnp.exp(jax.random.uniform(jax.random.fold_in(key, 42), (D,), jnp.float32, -1.15, 1.15))
    core = jnp.clip(jax.random.normal(jax.random.fold_in(key, 43), (REQUESTS, REQ_LEN, D), jnp.float32), -3.5, 3.5)
    return (core * row_scale * col_scale).astype(jnp.bfloat16)


def draw_queries(key, part):
    arr_shape = (REQUESTS, REQ_LEN, HEADS * HD)
    result = jnp.clip(1.5 * jax.random.normal(jax.random.fold_in(key, 1), arr_shape, jnp.float32), -8.0, 8.0)
    return result.astype(jnp.bfloat16)


def draw_fresh_kv(key, part):
    lead = (REQUESTS, REQ_LEN)
    key_part, value_part = key_value_rows(key, lead, 11)
    flat_keys = key_part.reshape(lead + (KVH * HD,))
    flat_values = value_part.reshape(lead + (KVH * HD,))
    return jnp.concatenate([flat_keys, flat_values], axis=-1).astype(jnp.bfloat16)


def draw_pool_cache(key, part):
    lead = (POOL_BLOCKS, BLOCK)
    key_part, value_part = key_value_rows(key, lead, 21)
    flat_keys = key_part.reshape(lead + (KVH * HD,))
    flat_values = value_part.reshape(lead + (KVH * HD,))
    return jnp.concatenate([flat_keys, flat_values], axis=-1).astype(jnp.bfloat16)


def draw_route_logits(key, part):
    arr_shape = (REQUESTS, REQ_LEN, TOPK)
    order_bits = jax.random.randint(jax.random.fold_in(key, 35), arr_shape, 0, 1 << 20).astype(jnp.int32) * TOPK + jnp.arange(TOPK, dtype=jnp.int32)
    ranks = jnp.argsort(jnp.argsort(order_bits, axis=-1), axis=-1)
    lowered = ranks < 2
    jitter = jnp.clip(0.1 * jax.random.normal(jax.random.fold_in(key, 31), arr_shape, jnp.float32), -0.3, 0.3)
    result = jnp.where(lowered, jitter - 2.0, jitter)
    return result.astype(jnp.float32)


def draw_hit_blocks(key, part):

    def draw_request(req_key):
        owner_order = jax.random.permutation(jax.random.fold_in(req_key, 1), N_POOL)
        hit_index = jnp.arange(HITS, dtype=jnp.int32)
        after_hot = jnp.maximum(hit_index - HOT, 0)
        others_pick = owner_order[1 + after_hot % (N_POOL - 1)]
        owners = jnp.where(hit_index < HOT, owner_order[0], others_pick)
        owner_rank = jnp.where(hit_index < HOT, hit_index, after_hot // (N_POOL - 1))
        perm_keys = jax.random.split(jax.random.fold_in(req_key, 2), N_POOL)
        local_perm = jax.vmap(lambda one_key: jax.random.permutation(one_key, PB_DEV))(perm_keys)
        local_index = local_perm[owners, owner_rank]
        block_ids = (owners * PB_DEV + local_index).astype(jnp.int32)
        return block_ids[jax.random.permutation(jax.random.fold_in(req_key, 3), HITS)]
    return jax.vmap(draw_request)(jax.random.split(key, REQUESTS)).astype(jnp.int32)


def block_levels(stream_key, extent, cuts, smallest, high):
    factor_of = 1.0
    for axis_at, blocks in cuts:
        heights = jax.random.uniform(jax.random.fold_in(jax.random.fold_in(stream_key, 6), axis_at), (blocks,), jnp.float32, smallest / len(cuts), high / len(cuts))
        factor_of = factor_of * jnp.repeat(jnp.exp(heights), extent[axis_at] // blocks).reshape((-1,) + (1,) * (len(extent) - 1 - axis_at))
    return factor_of


def deal_out(own_key, own, number, rows, amount, top, reach, skew):
    order = jax.random.permutation(own_key, amount)
    packed, ordinary = load_shares(amount, rows * top, reach, skew, True), load_shares(amount, rows * top, reach, skew, False)
    places = jnp.arange(amount)

    def named(sizes, offset_by):
        used = int((sizes > 0).sum())
        fixed = max(1, used // 4)
        shifted = fixed + (places - fixed + offset_by * (used - fixed)) % max(1, amount - fixed)
        return jnp.zeros((amount,), jnp.int32).at[order[jnp.where(places < fixed, places, shifted)]].set(jnp.asarray(sizes, jnp.int32))

    sizes = jnp.where(number % 4 == 0, named(packed, number // 4), named(ordinary, number - number // 4 - 1))
    mixed = jax.random.permutation(jax.random.fold_in(own, 3), amount)
    giver, receiver = mixed[0:amount // 2 * 2:2], mixed[1:amount // 2 * 2:2]
    margin = jnp.minimum(sizes[giver] - 1, reach - sizes[receiver]) // 2
    margin = jnp.where((giver == order[0]) | (receiver == order[0]) | (sizes[receiver] == 0), 0, jnp.maximum(margin, 0))
    shifted = jax.random.randint(jax.random.fold_in(own, 4), (amount // 2,), 0, 1 << 20) % (margin + 1)
    sizes = sizes.at[giver].add(-shifted).at[receiver].add(shifted)
    labels = jnp.searchsorted(jnp.cumsum(sizes), jnp.arange(rows * top), side="right").astype(jnp.int32)
    listing = labels.reshape(top, rows).T
    listing = listing[jax.random.permutation(jax.random.fold_in(own, 1), rows)]
    offset_by = jax.random.randint(jax.random.fold_in(own, 2), (rows, 1), 0, top)
    return jnp.take_along_axis(listing, (jnp.arange(top)[None, :] + offset_by) % top, axis=1)


def load_shares(amount, total, most, slope, full):
    weights = [(1 << 20) // math.isqrt(rank ** slope) + 1 for rank in range(1, amount + 1)]
    largest = most if full else min(most, max(-(-total // amount), total * weights[0] // sum(weights)))
    least = 1 if total - largest >= amount - 1 else 0
    holding, spare = [largest] + [least] * (amount - 1), total - largest - least * (amount - 1)
    while spare > 0:
        candidates = [i for i in range(1, amount) if holding[i] < largest] or [i for i in range(1, amount) if holding[i] < most]
        pool, budget = sum([weights[i] for i in candidates]), spare
        for i in candidates:
            more = min(most - holding[i], max(1, budget * weights[i] // pool), spare)
            holding[i] = holding[i] + more
            spare = spare - more
    return np.array(holding)


def bell_draw(own_key, shape, spread, most, cuts=(), kind=jnp.bfloat16):
    gain = block_levels(own_key, shape, cuts, -0.22, 0.18) if cuts else 1.0
    values = jax.random.normal(own_key, shape, jnp.float32) * spread * gain
    return jnp.minimum(jnp.maximum(values, -most), most).astype(kind)


def setup_inputs(seed: int = 0) -> dict:
    keys = jax.random.split(jax.random.key(seed), 12)
    residual = draw_residual(jax.random.fold_in(keys[11], 71), 0)
    queries = draw_queries(jax.random.fold_in(keys[11], 71), 0)
    fresh_kv = draw_fresh_kv(jax.random.fold_in(keys[11], 71), 0)
    pool_cache = draw_pool_cache(jax.random.fold_in(keys[11], 71), 0)
    hit_blocks = draw_hit_blocks(jax.random.fold_in(keys[11], 71), 0)
    norm_gain = jnp.clip(1.0 + 0.18 * jax.random.normal(keys[5], (D,), jnp.float32), 0.1, 1.9)
    route_ids_keys = jax.random.split(jax.random.fold_in(keys[6], 1), REQUESTS * REQ_LEN // TOK_DEV)
    route_ids_turns = jax.random.permutation(jax.random.fold_in(keys[6], 3), REQUESTS * REQ_LEN // TOK_DEV)
    route_ids = jax.vmap(lambda own, number: deal_out(jax.random.fold_in(keys[6], 2), own, number, TOK_DEV, EXPERTS, TOPK, MOST, 1))(route_ids_keys, route_ids_turns).reshape((REQUESTS, REQ_LEN, TOPK))
    route_logits = draw_route_logits(jax.random.fold_in(keys[11], 71), 0)
    w_gate = bell_draw(keys[8], (SLABS, D, HALF), (D // 8) ** -0.5, 0.25, ((0, 256),))
    w_up = bell_draw(keys[9], (SLABS, D, HALF), (D // 8) ** -0.5, 0.25, ((0, 256),))
    w_down = bell_draw(keys[10], (SLABS, HALF, D), (FFH // 8) ** -0.5, 0.625, ((0, 256),))
    return {"residual": residual, "queries": queries, "fresh_kv": fresh_kv, "pool_cache": pool_cache, "hit_blocks": hit_blocks, "norm_gain": norm_gain, "route_ids": route_ids, "route_logits": route_logits, "w_gate": w_gate, "w_up": w_up, "w_down": w_down}


MASKED = -1e+30
EPSILON = 1e-06

def attend_request(query_rows, new_rows, prefix_rows):
    group_size = HEADS // KVH
    key_rows = jnp.concatenate([prefix_rows, new_rows], axis=0)
    key_count = key_rows.shape[0]
    key_mat = key_rows[:, :KVH * HD].reshape(key_count, KVH, HD).astype(jnp.float32)
    values = key_rows[:, KVH * HD:].reshape(key_count, KVH, HD).astype(jnp.float32)
    query_heads = query_rows.reshape(REQ_LEN, KVH, group_size, HD).astype(jnp.float32)
    scores = jnp.einsum('tkgd,nkd->kgtn', query_heads, key_mat) * HD ** (-0.5)
    positions = jnp.arange(REQ_LEN, dtype=jnp.int32)
    key_pos = jnp.arange(key_count, dtype=jnp.int32) - HITS * BLOCK
    visible = key_pos[None, :] <= positions[:, None]
    scores = jnp.where(visible[None, None], scores, MASKED)
    row_max = lax.optimization_barrier(jnp.max(scores, axis=-1, keepdims=True))
    weights = jnp.where(visible[None, None], jnp.exp(scores - row_max), 0.0)
    row_sum = lax.optimization_barrier(jnp.sum(weights, axis=-1))
    rounded = lax.optimization_barrier(weights.astype(jnp.bfloat16)).astype(jnp.float32)
    attn_mix = jnp.einsum('kgtn,nkd->kgtd', rounded, values) / row_sum[..., None]
    return jnp.transpose(attn_mix, (2, 0, 1, 3)).reshape(REQ_LEN, HEADS * HD).astype(jnp.bfloat16)

def block_slots(block_routes):
    chosen = block_routes.reshape(-1)
    onehot = (chosen[:, None] == jnp.arange(EXPERTS, dtype=jnp.int32)[None, :]).astype(jnp.int32)
    ranking = lax.optimization_barrier(jnp.sum((jnp.cumsum(onehot, axis=0) - 1) * onehot, axis=1))
    slot_pos = chosen * MOST + ranking
    filler = jnp.arange(1, chosen.shape[0] + 1, dtype=jnp.int32)
    return jnp.zeros((EXPERTS * MOST,), jnp.int32).at[slot_pos].set(filler)

def reference(residual, queries, fresh_kv, pool_cache, hit_blocks, norm_gain, route_ids, route_logits, w_gate, w_up, w_down):

    def one_request(inputs):
        query_rows, new_rows, hit_list = inputs
        prefix_rows = pool_cache[hit_list].reshape(HITS * BLOCK, 2 * KVH * HD)
        return attend_request(query_rows, new_rows, prefix_rows)
    attended = lax.map(one_request, (queries, fresh_kv, hit_blocks))
    resid = lax.optimization_barrier((residual.astype(jnp.float32) + attended.astype(jnp.float32)).astype(jnp.bfloat16))
    resid_wide = resid.astype(jnp.float32)
    inv_rms = lax.rsqrt(lax.optimization_barrier(jnp.mean(resid_wide * resid_wide, axis=-1, keepdims=True)) + EPSILON)
    normed = (resid_wide * inv_rms * norm_gain).astype(jnp.bfloat16)
    normed_flat = normed.reshape(-1, D)
    route_weight = jax.nn.softmax(route_logits.astype(jnp.float32), axis=-1).reshape(-1)
    pair_blocks = route_ids.reshape(DEVICES, TOK_DEV, TOPK)
    tables = jax.vmap(block_slots)(pair_blocks)
    block_base = (jnp.arange(DEVICES, dtype=jnp.int32) * (TOK_DEV * TOPK))[:, None]
    tables = jnp.where(tables > 0, tables + block_base, 0)
    pair_table = jnp.transpose(tables.reshape(DEVICES, EXPERTS, MOST), (1, 0, 2)).reshape(EXPERTS, DEVICES * MOST)
    gate_pairs = w_gate.reshape(EXPERTS, 2, D, HALF)
    up_pairs = w_up.reshape(EXPERTS, 2, D, HALF)
    down_pairs = w_down.reshape(EXPERTS, 2, HALF, D)

    def expert_step(accum, inputs):
        pair_plus, gate_pair, up_pair, down_pair = inputs
        filled = pair_plus > 0
        pair_index = jnp.maximum(pair_plus - 1, 0)
        token_index = pair_index // TOPK
        expert_rows = jnp.where(filled[:, None], normed_flat[token_index], jnp.zeros((), normed_flat.dtype))
        combined = jnp.zeros((expert_rows.shape[0], D), jnp.float32)
        for half_index in range(2):
            gate_act = jnp.dot(expert_rows, gate_pair[half_index], preferred_element_type=jnp.float32)
            up_act = jnp.dot(expert_rows, up_pair[half_index], preferred_element_type=jnp.float32)
            hidden = (jax.nn.silu(gate_act) * up_act).astype(jnp.bfloat16)
            partial_value = jnp.dot(hidden, down_pair[half_index], preferred_element_type=jnp.float32).astype(jnp.bfloat16)
            combined = combined + lax.optimization_barrier(partial_value).astype(jnp.float32)
        coef = jnp.where(filled, route_weight[pair_index], 0.0)
        return (accum.at[token_index].add(coef[:, None] * combined), None)
    start_acc = jnp.zeros((REQUESTS * REQ_LEN, D), jnp.float32)
    expert_mix, unused = lax.scan(expert_step, start_acc, (pair_table, gate_pairs, up_pairs, down_pairs))
    layer_out = (resid_wide + expert_mix.reshape(REQUESTS, REQ_LEN, D)).astype(jnp.bfloat16)
    return (attended, layer_out)
```

```python
import jax
import jax.numpy as jnp
from jax import lax
from jax.experimental import pallas as pl
from jax.experimental.pallas import tpu as pltpu
from jax.sharding import Mesh, PartitionSpec as P

HD = 128
HOT = 4
MOST = 5
META = 128
MASKED = -1e30
EPSILON = 1e-06
F32 = jnp.float32
BF16 = jnp.bfloat16
VMEM_LIMIT = 56 * 1024 * 1024

SMEM = pl.BlockSpec(memory_space=pltpu.SMEM)
VMEM = pl.BlockSpec(memory_space=pltpu.VMEM)


def params(**kw):
    return pltpu.CompilerParams(vmem_limit_bytes=VMEM_LIMIT, **kw)


def gather_kernel(rank_ref, hit_ref, cache_ref, fresh_ref, ids_ref, logit_ref, out_ref):
    rank = rank_ref[0]
    held, block, width = cache_ref.shape
    out_ref[:, :width] = jnp.zeros((out_ref.shape[0], width), BF16)
    out_ref[:, width : 2 * width] = fresh_ref[...]
    count = jnp.int32(0)
    for i in range(hit_ref.shape[1]):
        hit = hit_ref[0, i]
        mine = lax.div(hit, held) == rank
        row = pl.multiple_of(jnp.minimum(count, HOT - 1) * block, block)
        local = lax.rem(hit, held)

        @pl.when(mine)
        def _():
            out_ref[pl.ds(row, block), :width] = cache_ref[local]

        count = count + mine.astype(jnp.int32)
    ids = ids_ref[...].astype(F32)
    logits = logit_ref[...]
    grown = jnp.exp(logits - jnp.max(logits, axis=-1, keepdims=True))
    weight = grown / jnp.sum(grown, axis=-1, keepdims=True)
    high = weight.astype(BF16).astype(F32)
    low = weight - high
    tok, top = ids.shape
    lane = lax.broadcasted_iota(jnp.int32, (tok, META), 1)
    meta = jnp.zeros((tok, META), F32)
    for part, values in enumerate((ids, high, low)):
        for j in range(top):
            meta = jnp.where(lane == part * top + j, values[:, j : j + 1], meta)
    out_ref[:, 2 * width :] = meta.astype(BF16)


def place_ring(rank, pools, tok, pieces, store):
    store(rank * tok, pieces[0][...])
    half = pools // 2
    for s in range(1, half):
        store(lax.rem(rank + pools - s, pools) * tok, pieces[2 * s - 1][...])
        store(lax.rem(rank + s, pools) * tok, pieces[2 * s][...])
    far = lax.rem(rank + half, pools) * tok
    store(far, pieces[2 * half - 1][...])
    store(far + tok // 2, pieces[2 * half][...])


def attend_kernel(rank_ref, hit_ref, gain_ref, query_ref, residual_ref, *refs, pools, held):
    pieces = refs[: pools + 1]
    attended_ref, resid_ref, normed_ref, meta_ref, part_ref, kv_ref, bias_ref = refs[pools + 1 :]
    rank = rank_ref[0]
    tok, model = query_ref.shape
    hits = hit_ref.shape[1]
    width = kv_ref.shape[1]
    block = tok // HOT

    def store(row, value):
        part_ref[pl.ds(pl.multiple_of(row, tok // 2), value.shape[0]), :] = value

    place_ring(rank, pools, tok, pieces, store)
    meta_ref[...] = part_ref[:, 2 * width :]
    owners = [lax.div(hit_ref[0, i], held) for i in range(hits)]
    for i in range(hits):
        slot = jnp.int32(0)
        for earlier in range(i):
            slot = slot + (owners[earlier] == owners[i]).astype(jnp.int32)
        row = pl.multiple_of(owners[i] * tok + jnp.minimum(slot, HOT - 1) * block, block)
        kv_ref[i * block : (i + 1) * block, :] = part_ref[pl.ds(row, block), :width]
    prefix = hits * block
    kv_ref[prefix:, :] = part_ref[:, width : 2 * width]
    heads_kv = width // (2 * HD)
    group = model // (heads_kv * HD)
    rows, keys = bias_ref.shape
    stack = rows // tok
    col = lax.broadcasted_iota(jnp.int32, (rows, keys), 1)
    position = lax.rem(lax.broadcasted_iota(jnp.int32, (rows, keys), 0), tok) + rank * tok
    bias_ref[...] = jnp.where(col - prefix <= position, 0.0, MASKED)
    squares = jnp.zeros((tok, HD), F32)
    for g in range(heads_kv):
        key_mat = kv_ref[:, g * HD : (g + 1) * HD]
        values = kv_ref[:, (heads_kv + g) * HD : (heads_kv + g + 1) * HD]
        for first in range(g * group, (g + 1) * group, stack):
            query = jnp.concatenate(
                [query_ref[:, h * HD : (h + 1) * HD] for h in range(first, first + stack)], axis=0
            )
            scores = lax.dot_general(
                query, key_mat, (((1,), (1,)), ((), ())), preferred_element_type=F32
            )
            scores = scores * HD ** (-0.5) + bias_ref[...]
            weights = jnp.exp(scores - jnp.max(scores, axis=-1, keepdims=True))
            row_sum = jnp.sum(weights, axis=-1, keepdims=True)
            mixed = jnp.dot(weights.astype(BF16), values, preferred_element_type=F32) / row_sum
            mixed = mixed.astype(BF16)
            for s in range(stack):
                cols = slice((first + s) * HD, (first + s + 1) * HD)
                part = mixed[s * tok : (s + 1) * tok]
                attended_ref[:, cols] = part
                resid = (residual_ref[:, cols].astype(F32) + part.astype(F32)).astype(BF16)
                resid_ref[:, cols] = resid
                wide = resid.astype(F32)
                squares = squares + wide * wide
    inv_rms = lax.rsqrt(jnp.sum(squares, axis=-1, keepdims=True) / model + EPSILON)
    normed_ref[...] = (resid_ref[...].astype(F32) * inv_rms * gain_ref[...]).astype(BF16)


def route_kernel(rank_ref, meta_ref, take_ref, high_ref, low_ref, *, pools, top):
    tokens = meta_ref.shape[0]
    slots = take_ref.shape[0]
    tok = tokens // pools
    per = pools * MOST
    first = rank_ref[0] * (slots // per)
    slot = lax.broadcasted_iota(jnp.int32, (tok, slots), 1)
    expert = (lax.div(slot, per) + first).astype(F32)
    inner = lax.rem(slot, per)
    of_block = lax.div(inner, MOST)
    place = lax.rem(inner, MOST).astype(F32)
    before = (
        lax.broadcasted_iota(jnp.int32, (tok, tok), 1)
        < lax.broadcasted_iota(jnp.int32, (tok, tok), 0)
    ).astype(F32)
    for b in range(pools):
        meta = meta_ref[b * tok : (b + 1) * tok, :].astype(F32)
        named = jnp.zeros((tok, slots), F32)
        high = jnp.zeros((tok, slots), F32)
        low = jnp.zeros((tok, slots), F32)
        for j in range(top):
            same = meta[:, j : j + 1] == expert
            named = jnp.where(same, 1.0, named)
            high = jnp.where(same, meta[:, top + j : top + j + 1], high)
            low = jnp.where(same, meta[:, 2 * top + j : 2 * top + j + 1], low)
        rank = jnp.dot(before.astype(BF16), named.astype(BF16), preferred_element_type=F32)
        chosen = (named > 0.5) & (rank == place) & (of_block == b)
        take_ref[:, b * tok : (b + 1) * tok] = jnp.where(chosen, 1.0, 0.0).T.astype(BF16)
        high_ref[b * tok : (b + 1) * tok, :] = jnp.where(chosen, high, 0.0).astype(BF16)
        low_ref[b * tok : (b + 1) * tok, :] = jnp.where(chosen, low, 0.0).astype(BF16)


def pack_kernel(rank_ref, take_ref, *refs, pools):
    pieces = refs[: pools + 1]
    out_ref, rows_ref = refs[pools + 1 :]
    tok = pieces[0].shape[0]

    def store(row, value):
        rows_ref[pl.ds(pl.multiple_of(row, tok // 2), value.shape[0]), :] = value

    place_ring(rank_ref[0], pools, tok, pieces, store)
    out_ref[...] = jnp.dot(
        take_ref[...], rows_ref[...], preferred_element_type=F32
    ).astype(BF16)


def expert_kernel(x_ref, g0, g1, u0, u1, d0, d1, out_ref, hidden_ref, *, steps, wide):
    i = pl.program_id(0)
    half = hidden_ref.shape[1] // 2

    def grow(gate_ref, up_ref, at):
        x = x_ref[...]
        gate = jnp.dot(x, gate_ref[...], preferred_element_type=F32)
        up = jnp.dot(x, up_ref[...], preferred_element_type=F32)
        hidden = gate / (1.0 + jnp.exp(-gate)) * up
        hidden_ref[:, at : at + wide] = hidden.astype(BF16)

    for s in range(steps):

        @pl.when(i == s)
        def _():
            grow(g0, u0, s * wide)

        @pl.when(i == steps + s)
        def _():
            grow(g1, u1, half + s * wide)

    @pl.when(i >= 2 * steps)
    def _():
        out_ref[...] = (
            jnp.dot(hidden_ref[:, :half], d0[...], preferred_element_type=F32)
            + jnp.dot(hidden_ref[:, half:], d1[...], preferred_element_type=F32)
        ).astype(BF16)


def mix_kernel(high_ref, low_ref, y_ref, out_ref):
    y = y_ref[...]
    out_ref[...] = (
        jnp.dot(high_ref[...], y, preferred_element_type=F32)
        + jnp.dot(low_ref[...], y, preferred_element_type=F32)
    ).astype(BF16)


def ring(block, pools):
    right = [(k, (k + 1) % pools) for k in range(pools)]
    left = [(k, (k - 1) % pools) for k in range(pools)]
    pieces = [block]
    from_left = from_right = block
    for _ in range(1, pools // 2):
        from_left = lax.ppermute(from_left, "pool", right)
        from_right = lax.ppermute(from_right, "pool", left)
        pieces += [from_left, from_right]
    half = block.shape[0] // 2
    pieces += [
        lax.ppermute(from_left[:half], "pool", right),
        lax.ppermute(from_right[half:], "pool", left),
    ]
    return pieces


def shards(
    residual,
    queries,
    fresh_kv,
    pool_cache,
    hit_blocks,
    norm_gain,
    route_ids,
    route_logits,
    w_gate,
    w_up,
    w_down,
):
    pools = lax.axis_size("pool")
    plane = lax.axis_size("xy")
    rank = lax.axis_index("pool").astype(jnp.int32)[None]
    _, tok, model = queries.shape
    held, block, width = pool_cache.shape
    hits = hit_blocks.shape[1]
    top = route_ids.shape[2]
    half = w_gate.shape[2]
    shape = jax.ShapeDtypeStruct

    swap = [(0, 1), (1, 0)]
    own = (w_gate[0], w_up[0], w_down[0])
    peer = tuple(lax.ppermute(w, "core", swap) for w in own)

    packed = pl.pallas_call(
        gather_kernel,
        in_specs=[SMEM, SMEM, VMEM, VMEM, VMEM, VMEM],
        out_specs=VMEM,
        out_shape=shape((tok, 2 * width + META), BF16),
        compiler_params=params(),
        name="gather_block",
    )(rank, hit_blocks, pool_cache, fresh_kv[0], route_ids[0], route_logits[0])
    pieces = ring(packed, pools)

    stack = 4
    keys = hits * block + pools * tok
    attended, resid, normed, meta = pl.pallas_call(
        lambda *refs: attend_kernel(*refs, pools=pools, held=held),
        in_specs=[SMEM, SMEM] + [VMEM] * (3 + pools + 1),
        out_specs=[VMEM] * 4,
        out_shape=[shape((tok, model), BF16)] * 3 + [shape((pools * tok, META), BF16)],
        scratch_shapes=[
            pltpu.VMEM((pools * tok, 2 * width + META), BF16),
            pltpu.VMEM((keys, width), BF16),
            pltpu.VMEM((stack * tok, keys), F32),
        ],
        compiler_params=params(),
        name="attend",
    )(rank, hit_blocks, norm_gain[None], queries[0], residual[0], *pieces)

    slots = plane * pools * MOST
    take, high, low = pl.pallas_call(
        lambda *refs: route_kernel(*refs, pools=pools, top=top),
        in_specs=[SMEM, VMEM],
        out_specs=[VMEM] * 3,
        out_shape=[shape((slots, pools * tok), BF16)] + [shape((pools * tok, slots), BF16)] * 2,
        compiler_params=params(),
        name="route",
    )(rank, meta)

    rows = ring(normed, pools)
    chunk = min(1024, model)
    outgoing = pl.pallas_call(
        lambda *refs: pack_kernel(*refs, pools=pools),
        grid=(model // chunk,),
        in_specs=[SMEM, pl.BlockSpec((slots, pools * tok), lambda i: (0, 0))]
        + [pl.BlockSpec((r.shape[0], chunk), lambda i: (0, i)) for r in rows],
        out_specs=pl.BlockSpec((slots, chunk), lambda i: (0, i)),
        out_shape=shape((slots, model), BF16),
        scratch_shapes=[pltpu.VMEM((pools * tok, chunk), BF16)],
        compiler_params=params(),
        name="pack",
    )(rank, take, *rows)
    per = slots // plane
    arrived = lax.all_to_all(
        outgoing.reshape(plane, per, model), "xy", split_axis=0, concat_axis=0, tiled=True
    ).reshape(slots, model)

    wide = min(128, half)
    steps = half // wide
    cols = min(1024, model)
    downs = model // cols
    y = pl.pallas_call(
        lambda *refs: expert_kernel(*refs, steps=steps, wide=wide),
        grid=(2 * steps + downs,),
        in_specs=[pl.BlockSpec((slots, model), lambda i: (0, 0))]
        + [
            pl.BlockSpec((model, wide), lambda i: (0, jnp.clip(i, 0, steps - 1))),
            pl.BlockSpec((model, wide), lambda i: (0, jnp.clip(i - steps, 0, steps - 1))),
        ]
        * 2
        + [pl.BlockSpec((half, cols), lambda i: (0, jnp.clip(i - 2 * steps, 0, downs - 1)))] * 2,
        out_specs=pl.BlockSpec((slots, cols), lambda i: (0, jnp.clip(i - 2 * steps, 0, downs - 1))),
        out_shape=shape((slots, model), BF16),
        scratch_shapes=[pltpu.VMEM((slots, 2 * half), BF16)],
        compiler_params=params(),
        name="expert",
    )(arrived, own[0], peer[0], own[1], peer[1], own[2], peer[2])

    returned = lax.all_to_all(
        y.reshape(plane, per, model), "xy", split_axis=0, concat_axis=0, tiled=True
    ).reshape(slots, model)
    mixed = pl.pallas_call(
        mix_kernel,
        grid=(model // chunk,),
        in_specs=[pl.BlockSpec((pools * tok, slots), lambda i: (0, 0))] * 2
        + [pl.BlockSpec((slots, chunk), lambda i: (0, i))],
        out_specs=pl.BlockSpec((pools * tok, chunk), lambda i: (0, i)),
        out_shape=shape((pools * tok, model), BF16),
        compiler_params=params(),
        name="mix",
    )(high, low, returned)
    mix = lax.psum_scatter(mixed, "pool", scatter_dimension=0, tiled=True)
    layer_out = (resid.astype(F32) + mix.astype(F32)).astype(BF16)
    return (attended[None], layer_out[None])


def solution(mesh):
    pools, experts = mesh.devices.shape
    fine = Mesh(mesh.devices.reshape(pools, experts // 2, 2), ("pool", "xy", "core"))
    ex = ("xy", "core")
    tokens = P(ex, "pool", None)
    slab = P(("pool", "xy", "core"), None, None)
    placed = (
        tokens,
        tokens,
        tokens,
        P("pool", None, None),
        P(ex, None),
        P(),
        tokens,
        tokens,
        slab,
        slab,
        slab,
    )
    return jax.shard_map(
        shards, mesh=fine, in_specs=placed, out_specs=(tokens, tokens), check_vma=False
    )
```

```python
import jax
import jax.numpy as jnp
from jax import lax
from jax.experimental import pallas as pl
from jax.experimental.pallas import tpu as pltpu
from jax.sharding import Mesh, PartitionSpec as P

HD = 128
HOT = 4
MOST = 5
META = 128
OFFSETS = (0, -1, 1, -2, 2, -3, 3, 4)
PARTS = (
    [(0, 0), (0, 1), (0, 2), (0, 3), (1, 0), (1, 1), (2, 0), (2, 1)],
    [(p, k) for p in (1, 2) for k in (2, 3, 4)] + [(p, k) for p in (3, 4) for k in range(MOST)],
    [(0, 4)] + [(p, k) for p in (5, 6, 7) for k in range(MOST)],
)
PIECES = ((0, 1, 2), (1, 2, 3, 4), (0, 5, 6, 7))
MASKED = -1e30
EPSILON = 1e-06
F32 = jnp.float32
BF16 = jnp.bfloat16
VMEM_LIMIT = 56 * 1024 * 1024

SMEM = pl.BlockSpec(memory_space=pltpu.SMEM)
VMEM = pl.BlockSpec(memory_space=pltpu.VMEM)


def params(**kw):
    return pltpu.CompilerParams(vmem_limit_bytes=VMEM_LIMIT, **kw)


def gather_kernel(rank_ref, hit_ref, cache_ref, fresh_ref, ids_ref, logit_ref, out_ref):
    rank = rank_ref[0]
    held, block, width = cache_ref.shape
    out_ref[:, :width] = jnp.zeros((out_ref.shape[0], width), BF16)
    out_ref[:, width : 2 * width] = fresh_ref[...]
    count = jnp.int32(0)
    for i in range(hit_ref.shape[1]):
        hit = hit_ref[0, i]
        mine = lax.div(hit, held) == rank
        row = pl.multiple_of(jnp.minimum(count, HOT - 1) * block, block)
        local = lax.rem(hit, held)

        @pl.when(mine)
        def _():
            out_ref[pl.ds(row, block), :width] = cache_ref[local]

        count = count + mine.astype(jnp.int32)
    ids = ids_ref[...].astype(F32).T
    logits = logit_ref[...].T
    grown = jnp.exp(logits - jnp.max(logits, axis=-1, keepdims=True))
    weight = grown / jnp.sum(grown, axis=-1, keepdims=True)
    high = weight.astype(BF16).astype(F32)
    low = weight - high
    tok, top = ids.shape
    lane = lax.broadcasted_iota(jnp.int32, (tok, META), 1)
    meta = jnp.zeros((tok, META), F32)
    for part, values in enumerate((ids, high, low)):
        for j in range(top):
            meta = jnp.where(lane == part * top + j, values[:, j : j + 1], meta)
    out_ref[:, 2 * width :] = meta.astype(BF16)


def place_ring(rank, pools, tok, pieces, store):
    store(rank * tok, pieces[0][...])
    half = pools // 2
    for s in range(1, half):
        store(lax.rem(rank + pools - s, pools) * tok, pieces[2 * s - 1][...])
        store(lax.rem(rank + s, pools) * tok, pieces[2 * s][...])
    far = lax.rem(rank + half, pools) * tok
    store(far, pieces[2 * half - 1][...])
    store(far + tok // 2, pieces[2 * half][...])


def attend_kernel(rank_ref, hit_ref, gain_ref, query_ref, residual_ref, *refs, pools, held):
    pieces = refs[: pools + 1]
    attended_ref, resid_ref, normed_ref, meta_ref, part_ref, kv_ref, bias_ref = refs[pools + 1 :]
    rank = rank_ref[0]
    tok, model = query_ref.shape
    hits = hit_ref.shape[1]
    width = kv_ref.shape[1]
    block = tok // HOT

    def store(row, value):
        part_ref[pl.ds(pl.multiple_of(row, tok // 2), value.shape[0]), :] = value

    place_ring(rank, pools, tok, pieces, store)
    meta_ref[...] = part_ref[:, 2 * width :]
    owners = [lax.div(hit_ref[0, i], held) for i in range(hits)]
    for i in range(hits):
        slot = jnp.int32(0)
        for earlier in range(i):
            slot = slot + (owners[earlier] == owners[i]).astype(jnp.int32)
        row = pl.multiple_of(owners[i] * tok + jnp.minimum(slot, HOT - 1) * block, block)
        kv_ref[i * block : (i + 1) * block, :] = part_ref[pl.ds(row, block), :width]
    prefix = hits * block
    kv_ref[prefix:, :] = part_ref[:, width : 2 * width]
    heads_kv = width // (2 * HD)
    group = model // (heads_kv * HD)
    rows, keys = bias_ref.shape
    stack = rows // tok
    col = lax.broadcasted_iota(jnp.int32, (rows, keys), 1)
    position = lax.rem(lax.broadcasted_iota(jnp.int32, (rows, keys), 0), tok) + rank * tok
    bias_ref[...] = jnp.where(col - prefix <= position, 0.0, MASKED)
    squares = jnp.zeros((tok, HD), F32)
    for g in range(heads_kv):
        key_mat = kv_ref[:, g * HD : (g + 1) * HD]
        values = kv_ref[:, (heads_kv + g) * HD : (heads_kv + g + 1) * HD]
        for first in range(g * group, (g + 1) * group, stack):
            query = jnp.concatenate(
                [query_ref[:, h * HD : (h + 1) * HD] for h in range(first, first + stack)], axis=0
            )
            scores = lax.dot_general(
                query, key_mat, (((1,), (1,)), ((), ())), preferred_element_type=F32
            )
            scores = scores * HD ** (-0.5) + bias_ref[...]
            weights = jnp.exp(scores - jnp.max(scores, axis=-1, keepdims=True))
            row_sum = jnp.sum(weights, axis=-1, keepdims=True)
            mixed = jnp.dot(weights.astype(BF16), values, preferred_element_type=F32) / row_sum
            mixed = mixed.astype(BF16)
            for s in range(stack):
                cols = slice((first + s) * HD, (first + s + 1) * HD)
                part = mixed[s * tok : (s + 1) * tok]
                attended_ref[:, cols] = part
                resid = (residual_ref[:, cols].astype(F32) + part.astype(F32)).astype(BF16)
                resid_ref[:, cols] = resid
                wide = resid.astype(F32)
                squares = squares + wide * wide
    inv_rms = lax.rsqrt(jnp.sum(squares, axis=-1, keepdims=True) / model + EPSILON)
    normed_ref[...] = (resid_ref[...].astype(F32) * inv_rms * gain_ref[...]).astype(BF16)


def route_kernel(rank_ref, meta_ref, *refs, pools, top):
    tok = meta_ref.shape[0] // pools
    rank = rank_ref[0]
    takes, mixes = refs[: len(PARTS)], refs[len(PARTS) :]
    before = (
        lax.broadcasted_iota(jnp.int32, (tok, tok), 1)
        < lax.broadcasted_iota(jnp.int32, (tok, tok), 0)
    ).astype(BF16)
    for part, pieces, take_ref, mix_ref in zip(PARTS, PIECES, takes, mixes):
        slots = take_ref.shape[0]
        per = len(part)
        plane = slots // per
        slot = lax.broadcasted_iota(jnp.int32, (tok, slots), 1)
        inner = lax.rem(slot, per)
        expert = (lax.div(slot, per) + rank * plane).astype(F32)
        for at, piece in enumerate(pieces):
            place = jnp.full((tok, slots), -1, jnp.int32)
            for n, (p, k) in enumerate(part):
                if p == piece:
                    place = jnp.where(inner == n, k, place)
            row = lax.rem(rank + pools + OFFSETS[piece], pools) * tok
            meta = meta_ref[pl.ds(pl.multiple_of(row, tok), tok), :].astype(F32)
            named = jnp.zeros((tok, slots), F32)
            high = jnp.zeros((tok, slots), F32)
            low = jnp.zeros((tok, slots), F32)
            for j in range(top):
                same = meta[:, j : j + 1] == expert
                named = jnp.where(same, 1.0, named)
                high = jnp.where(same, meta[:, top + j : top + j + 1], high)
                low = jnp.where(same, meta[:, 2 * top + j : 2 * top + j + 1], low)
            count = jnp.dot(before, named.astype(BF16), preferred_element_type=F32)
            chosen = (named > 0.5) & (count == place.astype(F32))
            here = slice(at * tok, (at + 1) * tok)
            take_ref[:, here] = jnp.where(chosen, 1.0, 0.0).T.astype(BF16)
            mix_ref[0, here, :] = jnp.where(chosen, high, 0.0).astype(BF16)
            mix_ref[1, here, :] = jnp.where(chosen, low, 0.0).astype(BF16)


def pack_kernel(take_ref, *refs):
    pieces, (out_ref, rows_ref) = refs[:-2], refs[-2:]
    at = 0
    for piece in pieces:
        rows_ref[at : at + piece.shape[0], :] = piece[...]
        at += piece.shape[0]
    out_ref[...] = jnp.dot(take_ref[...], rows_ref[...], preferred_element_type=F32).astype(BF16)


def expert_kernel(*refs, steps, count):
    xs, (g0, g1, u0, u1, d0, d1) = refs[:count], refs[count : count + 6]
    outs, (x_ref, sum_ref, hidden_ref) = refs[count + 6 : 2 * count + 6], refs[2 * count + 6 :]
    i = pl.program_id(0)
    half = g0.shape[1]
    if count == 1:
        x_ref = xs[0]

    @pl.when(i < steps)
    def _():
        at = 0
        for x in xs if count > 1 else ():
            x_ref[at : at + x.shape[0], :] = x[...]
            at += x.shape[0]

    @pl.when(i == 0)
    def _():
        for at, w_ref in enumerate((g0, u0, g1, u1)):
            sum_ref[at] = jnp.dot(x_ref[...], w_ref[...], preferred_element_type=F32)

    @pl.when((i > 0) & (i < steps))
    def _():
        for at, w_ref in enumerate((g0, u0, g1, u1)):
            sum_ref[at] += jnp.dot(x_ref[...], w_ref[...], preferred_element_type=F32)

    @pl.when(i == steps - 1)
    def _():
        for at in range(2):
            gate, up = sum_ref[2 * at], sum_ref[2 * at + 1]
            hidden = gate / (1.0 + jnp.exp(-gate)) * up
            hidden_ref[:, at * half : (at + 1) * half] = hidden.astype(BF16)

    @pl.when(i >= steps)
    def _():
        y = (
            jnp.dot(hidden_ref[:, :half], d0[...], preferred_element_type=F32)
            + jnp.dot(hidden_ref[:, half:], d1[...], preferred_element_type=F32)
        ).astype(BF16)
        at = 0
        for out in outs:
            out[...] = y[at : at + out.shape[0]]
            at += out.shape[0]


def weighted(mix_ref, first, last, y):
    return jnp.dot(mix_ref[0, first:last, :], y, preferred_element_type=F32) + jnp.dot(
        mix_ref[1, first:last, :], y, preferred_element_type=F32
    )


def far_kernel(mix_ref, y_ref, near_mix_ref, near_y_ref, resid_ref, own_ref, first_ref, third_ref, fourth_ref):
    tok = own_ref.shape[0]
    far = weighted(mix_ref, 0, 4 * tok, y_ref[...])
    near = weighted(near_mix_ref, 0, 3 * tok, near_y_ref[...])
    own_ref[...] = far[:tok] + near[:tok] + resid_ref[...].astype(F32)
    first_ref[...] = near[tok:]
    third_ref[...] = far[tok : 3 * tok]
    fourth_ref[...] = far[3 * tok :].astype(BF16)


def third_kernel(third_ref, from_left_ref, from_right_ref, right_ref, left_ref):
    tok = right_ref.shape[0]
    half = tok // 2
    right_ref[:half] = (third_ref[tok : tok + half] + from_left_ref[...].astype(F32)).astype(BF16)
    right_ref[half:] = third_ref[tok + half :].astype(BF16)
    left_ref[:half] = third_ref[:half].astype(BF16)
    left_ref[half:] = (third_ref[half:tok] + from_right_ref[...].astype(F32)).astype(BF16)


def second_kernel(mix_ref, y_ref, from_left_ref, from_right_ref, right_ref, left_ref):
    tok = right_ref.shape[0]
    mixed = weighted(mix_ref, 2 * tok, 4 * tok, y_ref[...])
    left_ref[...] = (mixed[:tok] + from_right_ref[...].astype(F32)).astype(BF16)
    right_ref[...] = (mixed[tok:] + from_left_ref[...].astype(F32)).astype(BF16)


def first_kernel(mix_ref, y_ref, first_ref, out_ref):
    out_ref[...] = first_ref[...] + weighted(mix_ref, 0, first_ref.shape[0], y_ref[...])


def ring(block, pools):
    right = [(k, (k + 1) % pools) for k in range(pools)]
    left = [(k, (k - 1) % pools) for k in range(pools)]
    pieces = [block]
    from_left = from_right = block
    for _ in range(1, pools // 2):
        from_left = lax.ppermute(from_left, "pool", right)
        from_right = lax.ppermute(from_right, "pool", left)
        pieces += [from_left, from_right]
    half = block.shape[0] // 2
    pieces += [
        lax.ppermute(from_left[:half], "pool", right),
        lax.ppermute(from_right[half:], "pool", left),
    ]
    return pieces


def shards(
    residual,
    queries,
    fresh_kv,
    pool_cache,
    hit_blocks,
    norm_gain,
    route_ids,
    route_logits,
    w_gate,
    w_up,
    w_down,
):
    pools = lax.axis_size("pool")
    plane = lax.axis_size("xy")
    rank = lax.axis_index("pool").astype(jnp.int32)[None]
    _, tok, model = queries.shape
    held, block, width = pool_cache.shape
    hits = hit_blocks.shape[1]
    top = route_ids.shape[2]
    half = w_gate.shape[2]
    shape = jax.ShapeDtypeStruct

    swap = [(0, 1), (1, 0)]
    own = (w_gate[0], w_up[0], w_down[0])
    peer = tuple(lax.ppermute(w, "core", swap) for w in own)

    packed = pl.pallas_call(
        gather_kernel,
        in_specs=[SMEM, SMEM, VMEM, VMEM, VMEM, VMEM],
        out_specs=VMEM,
        out_shape=shape((tok, 2 * width + META), BF16),
        compiler_params=params(),
        name="gather_block",
    )(rank, hit_blocks, pool_cache, fresh_kv[0], route_ids[0].T, route_logits[0].T)
    pieces = ring(packed, pools)
    pieces, peer = lax.optimization_barrier((pieces, peer))

    stack = 4
    keys = hits * block + pools * tok
    attended, resid, normed, meta = pl.pallas_call(
        lambda *refs: attend_kernel(*refs, pools=pools, held=held),
        in_specs=[SMEM, SMEM] + [VMEM] * (3 + pools + 1),
        out_specs=[VMEM] * 4,
        out_shape=[shape((tok, model), BF16)] * 3 + [shape((pools * tok, META), BF16)],
        scratch_shapes=[
            pltpu.VMEM((pools * tok, 2 * width + META), BF16),
            pltpu.VMEM((keys, width), BF16),
            pltpu.VMEM((stack * tok, keys), F32),
        ],
        compiler_params=params(),
        name="attend",
    )(rank, hit_blocks, norm_gain[None], queries[0], residual[0], *pieces)

    sizes = [(plane * len(part), tok * len(at)) for part, at in zip(PARTS, PIECES)]
    routed = pl.pallas_call(
        lambda *refs: route_kernel(*refs, pools=pools, top=top),
        in_specs=[SMEM, VMEM],
        out_specs=[VMEM] * 6,
        out_shape=[shape((slots, rows), BF16) for slots, rows in sizes]
        + [shape((2, rows, slots), BF16) for slots, rows in sizes],
        compiler_params=params(),
        name="route",
    )(rank, meta)
    takes, mixes = routed[:3], routed[3:]

    chunk = min(1024, model)
    whole = lambda x: pl.BlockSpec(x.shape, lambda i: (0,) * x.ndim)
    part = lambda rows: pl.BlockSpec((rows, chunk), lambda i: (0, i))

    def pack(take, parts, name):
        slots, rows = take.shape
        out = pl.pallas_call(
            pack_kernel,
            grid=(model // chunk,),
            in_specs=[whole(take)] + [part(p.shape[0]) for p in parts],
            out_specs=part(slots),
            out_shape=shape((slots, model), BF16),
            scratch_shapes=[pltpu.VMEM((rows, chunk), BF16)],
            compiler_params=params(),
            name=name,
        )(take, *parts)
        return out

    def exchange(x):
        slots = x.shape[0]
        x = x.reshape(plane, slots // plane, model)
        return lax.all_to_all(x, "xy", split_axis=0, concat_axis=0, tiled=True).reshape(
            slots, model
        )

    deep = min(1024, model)
    steps = model // deep
    cols = min(1024, model)
    downs = model // cols

    def expert(xs, name):
        slots = [x.shape[0] for x in xs]
        grown = lambda i: jnp.minimum(i, steps - 1)
        down = lambda i: (0, jnp.maximum(i - steps, 0))
        return pl.pallas_call(
            lambda *refs: expert_kernel(*refs, steps=steps, count=len(xs)),
            grid=(steps + downs,),
            in_specs=[pl.BlockSpec((n, deep), lambda i: (0, grown(i))) for n in slots]
            + [pl.BlockSpec((deep, half), lambda i: (grown(i), 0))] * 4
            + [pl.BlockSpec((half, cols), down)] * 2,
            out_specs=[pl.BlockSpec((n, cols), down) for n in slots],
            out_shape=[shape((n, model), BF16) for n in slots],
            scratch_shapes=[
                pltpu.VMEM((sum(slots), deep), BF16),
                pltpu.VMEM((4, sum(slots), half), F32),
                pltpu.VMEM((sum(slots), 2 * half), BF16),
            ],
            compiler_params=params(),
            name=name,
        )(*xs, own[0], peer[0], own[1], peer[1], own[2], peer[2])

    right = [(k, (k + 1) % pools) for k in range(pools)]
    left = [(k, (k - 1) % pools) for k in range(pools)]
    send = lambda r, l: (lax.ppermute(r, "pool", right), lax.ppermute(l, "pool", left))
    tie = lax.optimization_barrier

    once = send(normed, normed)
    once, takes = tie((once, takes))
    twice = send(*once)
    thrice = send(*twice)
    fourth = send(thrice[0][: tok // 2], thrice[1][tok // 2 :])
    sent_first = pack(takes[0], [normed, *once], "pack_first")
    sent_mid = pack(takes[1], [*once, *twice], "pack_mid")
    sent_far = pack(takes[2], [normed, *thrice, *fourth], "pack_far")
    got_first = exchange(sent_first)
    got_first, sent_mid = tie((got_first, sent_mid))
    got_mid = exchange(sent_mid)
    got_mid, sent_far = tie((got_mid, sent_far))
    got_far = exchange(sent_far)
    out_first, out_mid = expert([got_first, got_mid], "expert_near")
    got_far, out_first, out_mid = tie((got_far, out_first, out_mid))
    back_first = exchange(out_first)
    (out_far,) = expert([got_far], "expert_far")
    out_far, back_first = tie((out_far, back_first))
    back_far = exchange(out_far)
    out_mid, back_far = tie((out_mid, back_far))
    back_mid = exchange(out_mid)

    base, first, third, fourth = pl.pallas_call(
        far_kernel,
        grid=(model // chunk,),
        in_specs=[
            whole(mixes[2]),
            part(sizes[2][0]),
            whole(mixes[0]),
            part(sizes[0][0]),
            part(tok),
        ],
        out_specs=[part(tok), part(2 * tok), part(2 * tok), part(tok)],
        out_shape=[
            shape((tok, model), F32),
            shape((2 * tok, model), F32),
            shape((2 * tok, model), F32),
            shape((tok, model), BF16),
        ],
        compiler_params=params(),
        name="mix_far",
    )(mixes[2], back_far, mixes[0], back_first, resid)
    moving = send(fourth[: tok // 2], fourth[tok // 2 :])
    moving = pl.pallas_call(
        third_kernel,
        out_shape=[shape((tok, model), BF16)] * 2,
        compiler_params=params(),
        name="add_third",
    )(third, *moving)
    moving = send(*moving)
    moving = pl.pallas_call(
        second_kernel,
        grid=(model // chunk,),
        in_specs=[whole(mixes[1]), part(sizes[1][0]), part(tok), part(tok)],
        out_specs=[part(tok)] * 2,
        out_shape=[shape((tok, model), BF16)] * 2,
        compiler_params=params(),
        name="mix_second",
    )(mixes[1], back_mid, *moving)
    moving = send(*moving)
    first = pl.pallas_call(
        first_kernel,
        grid=(model // chunk,),
        in_specs=[whole(mixes[1]), part(sizes[1][0]), part(2 * tok)],
        out_specs=part(2 * tok),
        out_shape=shape((2 * tok, model), F32),
        compiler_params=params(),
        name="mix_first",
    )(mixes[1], back_mid, first)
    moving = send(
        (first[tok:] + moving[0].astype(F32)).astype(BF16),
        (first[:tok] + moving[1].astype(F32)).astype(BF16),
    )
    layer_out = (base + moving[0].astype(F32) + moving[1].astype(F32)).astype(BF16)
    return (attended[None], layer_out[None])


def solution(mesh):
    pools, experts = mesh.devices.shape
    fine = Mesh(mesh.devices.reshape(pools, experts // 2, 2), ("pool", "xy", "core"))
    ex = ("xy", "core")
    tokens = P(ex, "pool", None)
    slab = P(("pool", "xy", "core"), None, None)
    placed = (
        tokens,
        tokens,
        tokens,
        P("pool", None, None),
        P(ex, None),
        P(),
        tokens,
        tokens,
        slab,
        slab,
        slab,
    )
    return jax.shard_map(
        shards, mesh=fine, in_specs=placed, out_specs=(tokens, tokens), check_vma=False
    )
```

```python
import jax
import jax.numpy as jnp
from jax import lax
from jax.experimental import pallas as pl
from jax.experimental.pallas import tpu as pltpu
from jax.sharding import Mesh, PartitionSpec as P

HD = 128
HOT = 4
MOST = 5
META = 128
NEAR = 5
NEAR_SLOTS = 24
FAR_SLOTS = 16
MASKED = -1e30
EPSILON = 1e-06
F32 = jnp.float32
BF16 = jnp.bfloat16
COLS = 1024

SMEM = pl.BlockSpec(memory_space=pltpu.SMEM)
VMEM = pl.BlockSpec(memory_space=pltpu.VMEM)
ANY = pl.BlockSpec(memory_space=pl.ANY)


class Fetched(tuple):
    pass


def in_hbm(x):
    return (pltpu.with_memory_space_constraint(x, pltpu.HBM),)


def held_call(kernel, name, outs, args, scalars=0, near=(), far=(), scratch=(), limit=56):
    given = list(args[:scalars])
    specs = [SMEM] * scalars
    for arg in args[scalars:]:
        if isinstance(arg, tuple):
            given.append(arg[0])
            specs.append(VMEM if isinstance(arg, Fetched) else ANY)
        else:
            given.append(pltpu.with_memory_space_constraint(arg, pltpu.VMEM))
            specs.append(VMEM)
    return pl.pallas_call(
        kernel,
        in_specs=specs,
        out_specs=[ANY if n in far else VMEM for n in range(len(outs))],
        out_shape=[
            pltpu.VMEM(o.shape, o.dtype) if n in near else o for n, o in enumerate(outs)
        ],
        scratch_shapes=list(scratch),
        compiler_params=pltpu.CompilerParams(vmem_limit_bytes=limit * 1024 * 1024),
        name=name,
    )(*given)


def gather_kernel(rank_ref, hit_ref, cache_ref, fresh_ref, ids_ref, logit_ref, out_ref, sem):
    rank = rank_ref[0]
    held, block, width = cache_ref.shape
    count = jnp.int32(0)
    local = [jnp.int32(0)] * HOT
    for i in range(hit_ref.shape[1]):
        hit = hit_ref[0, i]
        mine = lax.div(hit, held) == rank
        for slot in range(HOT):
            local[slot] = jnp.where(mine & (count == slot), lax.rem(hit, held), local[slot])
        count = count + mine.astype(jnp.int32)
    copies = [
        pltpu.make_async_copy(
            cache_ref.at[local[slot]],
            out_ref.at[slot * block : (slot + 1) * block, :width],
            sem.at[slot],
        )
        for slot in range(HOT)
    ]
    for copy in copies:
        copy.start()
    out_ref[:, width : 2 * width] = fresh_ref[...]
    ids = ids_ref[...].astype(F32).T
    logits = logit_ref[...].T
    grown = jnp.exp(logits - jnp.max(logits, axis=-1, keepdims=True))
    weight = grown / jnp.sum(grown, axis=-1, keepdims=True)
    high = weight.astype(BF16).astype(F32)
    low = weight - high
    tok, top = ids.shape
    lane = lax.broadcasted_iota(jnp.int32, (tok, META), 1)
    meta = jnp.zeros((tok, META), F32)
    for part, values in enumerate((ids, high, low)):
        for j in range(top):
            meta = jnp.where(lane == part * top + j, values[:, j : j + 1], meta)
    out_ref[:, 2 * width :] = meta.astype(BF16)
    for copy in copies:
        copy.wait()


def place_ring(rank, pools, tok, pieces, store):
    store(rank * tok, pieces[0][...])
    half = pools // 2
    for s in range(1, half):
        store(lax.rem(rank + pools - s, pools) * tok, pieces[2 * s - 1][...])
        store(lax.rem(rank + s, pools) * tok, pieces[2 * s][...])
    far = lax.rem(rank + half, pools) * tok
    store(far, pieces[2 * half - 1][...])
    store(far + tok // 2, pieces[2 * half][...])


def attend_kernel(rank_ref, hit_ref, gain_ref, query_ref, residual_ref, *refs, pools, held):
    pieces = refs[: pools + 1]
    attended_ref, resid_ref, normed_ref, meta_ref, part_ref, kv_ref, bias_ref = refs[pools + 1 :]
    rank = rank_ref[0]
    tok, model = query_ref.shape
    hits = hit_ref.shape[1]
    width = kv_ref.shape[1]
    block = tok // HOT

    def store(row, value):
        part_ref[pl.ds(pl.multiple_of(row, tok // 2), value.shape[0]), :] = value

    place_ring(rank, pools, tok, pieces, store)
    meta_ref[...] = part_ref[:, 2 * width :]
    owners = [lax.div(hit_ref[0, i], held) for i in range(hits)]
    for i in range(hits):
        slot = jnp.int32(0)
        for earlier in range(i):
            slot = slot + (owners[earlier] == owners[i]).astype(jnp.int32)
        row = pl.multiple_of(owners[i] * tok + jnp.minimum(slot, HOT - 1) * block, block)
        kv_ref[i * block : (i + 1) * block, :] = part_ref[pl.ds(row, block), :width]
    prefix = hits * block
    kv_ref[prefix:, :] = part_ref[:, width : 2 * width]
    heads_kv = width // (2 * HD)
    group = model // (heads_kv * HD)
    rows, keys = bias_ref.shape
    stack = rows // tok
    col = lax.broadcasted_iota(jnp.int32, (rows, keys), 1)
    position = lax.rem(lax.broadcasted_iota(jnp.int32, (rows, keys), 0), tok) + rank * tok
    bias_ref[...] = jnp.where(col - prefix <= position, 0.0, MASKED)

    def some_heads(n, squares):
        lane = lambda at: pl.ds(pl.multiple_of(at * HD, HD), HD)
        first = n * stack
        g = lax.div(first, group)
        query = jnp.concatenate([query_ref[:, lane(first + h)] for h in range(stack)], axis=0)
        scores = lax.dot_general(
            query, kv_ref[:, lane(g)], (((1,), (1,)), ((), ())), preferred_element_type=F32
        )
        scores = scores * HD ** (-0.5) + bias_ref[...]
        weights = jnp.exp(scores - jnp.max(scores, axis=-1, keepdims=True))
        row_sum = jnp.sum(weights, axis=-1, keepdims=True)
        mixed = jnp.dot(
            weights.astype(BF16), kv_ref[:, lane(heads_kv + g)], preferred_element_type=F32
        )
        mixed = (mixed / row_sum).astype(BF16)
        for h in range(stack):
            part = mixed[h * tok : (h + 1) * tok]
            attended_ref[:, lane(first + h)] = part
            wide = residual_ref[:, lane(first + h)].astype(F32) + part.astype(F32)
            resid = wide.astype(BF16)
            resid_ref[:, lane(first + h)] = resid
            wide = resid.astype(F32)
            squares = squares + wide * wide
        return squares

    squares = lax.fori_loop(
        0,
        model // (2 * stack * HD),
        lambda n, squares: some_heads(2 * n + 1, some_heads(2 * n, squares)),
        jnp.zeros((tok, HD), F32),
    )
    inv_rms = lax.rsqrt(jnp.sum(squares, axis=-1, keepdims=True) / model + EPSILON)
    normed_ref[...] = (resid_ref[...].astype(F32) * inv_rms * gain_ref[...]).astype(BF16)


def offset_of(piece):
    far = lax.div(piece + 1, 2)
    return jnp.where((lax.rem(piece, 2) == 1) & (piece < 7), -far, far)


def route_kernel(
    rank_ref, meta_ref, take_near_ref, take_far_ref, mix_near_ref, mix_far_ref, named_ref, *, pools, top
):
    tok = meta_ref.shape[0] // pools
    rank = rank_ref[0]
    plane = take_near_ref.shape[0] // NEAR_SLOTS
    before = (
        lax.broadcasted_iota(jnp.int32, (tok, tok), 1)
        < lax.broadcasted_iota(jnp.int32, (tok, tok), 0)
    ).astype(BF16)
    for near, per, take_ref, mix_ref in (
        (True, NEAR_SLOTS, take_near_ref, mix_near_ref),
        (False, FAR_SLOTS, take_far_ref, mix_far_ref),
    ):
        slots, rows = take_ref.shape
        slot = lax.broadcasted_iota(jnp.int32, (1, slots), 1)
        inner = lax.rem(slot, per)
        shared = (per // MOST) * MOST
        expert = (lax.div(slot, per) + rank * plane).astype(F32)
        of_piece = jnp.where(inner < shared, lax.div(inner, MOST) + (1 if near else NEAR), 0)
        own_place = inner - shared if near else MOST - 1
        place = jnp.where(inner < shared, lax.rem(inner, MOST), own_place).astype(F32)

        def one_piece(at, carry):
            piece = at if near else jnp.where(at == 0, 0, at + NEAR - 1)
            row = lax.rem(rank + pools + offset_of(piece), pools) * tok
            meta = meta_ref[pl.ds(pl.multiple_of(row, tok), tok), :].astype(F32)
            named = jnp.zeros((tok, slots), F32)
            high = jnp.zeros((tok, slots), F32)
            low = jnp.zeros((tok, slots), F32)
            for j in range(top):
                same = meta[:, j : j + 1] == expert
                named = jnp.where(same, 1.0, named)
                high = jnp.where(same, meta[:, top + j : top + j + 1], high)
                low = jnp.where(same, meta[:, 2 * top + j : 2 * top + j + 1], low)
            count = jnp.dot(before, named.astype(BF16), preferred_element_type=F32)
            chosen = (named > 0.5) & (count == jnp.where(of_piece == piece, place, -1.0))
            here = pl.ds(pl.multiple_of(at * tok, tok), tok)
            named_ref[here, :slots] = jnp.where(chosen, 1.0, 0.0)
            mix_ref[0, here, :] = jnp.where(chosen, high, 0.0).astype(BF16)
            mix_ref[1, here, :] = jnp.where(chosen, low, 0.0).astype(BF16)
            return carry

        lax.fori_loop(0, rows // tok, one_piece, 0)
        take_ref[...] = named_ref[:rows, :slots].T.astype(BF16)


def by_columns(width, body):
    def step(n, carry):
        body(pl.ds(pl.multiple_of(n * COLS, COLS), COLS))
        return carry

    lax.fori_loop(0, width // COLS, step, 0)


def pack_kernel(take_ref, *refs):
    pieces, (out_ref, rows_ref, packed_ref, sem) = refs[:-4], refs[-4:]
    wide = packed_ref.shape[2]

    def leave(n):
        cols = pl.ds(pl.multiple_of(n * wide, wide), wide)
        return pltpu.make_async_copy(packed_ref.at[n], out_ref.at[:, cols], sem.at[n])

    def step(n, carry):
        cols = pl.ds(pl.multiple_of(n * wide, wide), wide)
        at = 0
        for piece in pieces:
            rows_ref[at : at + piece.shape[0], :] = piece[:, cols]
            at += piece.shape[0]
        packed_ref[n] = jnp.dot(
            take_ref[...], rows_ref[...], preferred_element_type=F32
        ).astype(BF16)
        leave(n).start()
        return carry

    parts = sem.shape[0]
    lax.fori_loop(0, parts, step, 0)
    for n in range(parts):
        leave(n).wait()


def expert_kernel(
    x, g0, g1, u0, u1, d0, d1, out, x_ref, grow_ref, down_ref, sum_ref, hidden_ref, y_ref, x_sem, grow_sem, down_sem, out_sem
):
    half = g0.shape[1]
    parts = x_sem.shape[0]
    deep = x.shape[1] // parts
    ends = out_sem.shape[0]
    wide = out.shape[1] // ends

    def row_copy(n):
        cols = pl.ds(pl.multiple_of(n * deep, deep), deep)
        return pltpu.make_async_copy(x.at[:, cols], x_ref.at[:, cols], x_sem.at[n])

    def grow_copies(slab, n, gate, up):
        rows = pl.ds(pl.multiple_of(n * deep, deep), deep)
        return [
            pltpu.make_async_copy(
                w.at[rows, :],
                grow_ref.at[slab, rows, pl.ds(at * half, half)],
                grow_sem.at[slab, n, at],
            )
            for at, w in enumerate((gate, up))
        ]

    def down_copies(n):
        cols = pl.ds(pl.multiple_of(n * wide, wide), wide)
        return [
            pltpu.make_async_copy(
                w.at[:, cols], down_ref.at[n, pl.ds(at * half, half), :], down_sem.at[n, at]
            )
            for at, w in enumerate((d0, d1))
        ]

    def leave(n):
        cols = pl.ds(pl.multiple_of(n * wide, wide), wide)
        return pltpu.make_async_copy(y_ref.at[n], out.at[:, cols], out_sem.at[n])

    for slab, (gate, up) in enumerate(((g0, u0), (g1, u1))):
        for n in range(parts):
            if slab == 0:
                row_copy(n).start()
            for copy in grow_copies(slab, n, gate, up):
                copy.start()
    for n in range(ends):
        for copy in down_copies(n):
            copy.start()

    def grow(step, carry):
        slab, n = lax.div(step, parts), lax.rem(step, parts)

        @pl.when(slab == 0)
        def _():
            row_copy(n).wait()

        for copy in grow_copies(slab, n, g0, u0):
            copy.wait()
        part = pl.ds(pl.multiple_of(n * deep, deep), deep)
        grown = jnp.dot(x_ref[:, part], grow_ref[slab, part, :], preferred_element_type=F32)
        sum_ref[slab] += grown
        return carry

    sum_ref[...] = jnp.zeros(sum_ref.shape, F32)
    lax.fori_loop(0, 2 * parts, grow, 0)
    for slab in range(2):
        gate, up = sum_ref[slab, :, :half], sum_ref[slab, :, half:]
        hidden = gate / (1.0 + jnp.exp(-gate)) * up
        hidden_ref[:, slab * half : (slab + 1) * half] = hidden.astype(BF16)

    def shrink(n, carry):
        for copy in down_copies(n):
            copy.wait()
        y_ref[n] = jnp.dot(
            hidden_ref[...], down_ref[n], preferred_element_type=F32
        ).astype(BF16)
        leave(n).start()
        return carry

    lax.fori_loop(0, ends, shrink, 0)
    for n in range(ends):
        leave(n).wait()


def weighted(mix_ref, first, last, y):
    return jnp.dot(mix_ref[0, first:last, :], y, preferred_element_type=F32) + jnp.dot(
        mix_ref[1, first:last, :], y, preferred_element_type=F32
    )


def far_kernel(mix_ref, y_ref, own_ref, third_ref, right_ref, left_ref):
    tok = own_ref.shape[0]
    half = tok // 2

    def body(cols):
        mixed = weighted(mix_ref, 0, mix_ref.shape[1], y_ref[:, cols])
        own_ref[:, cols] = mixed[:tok]
        third_ref[:, cols] = mixed[tok : 3 * tok]
        right_ref[:, cols] = mixed[3 * tok : 3 * tok + half].astype(BF16)
        left_ref[:, cols] = mixed[3 * tok + half :].astype(BF16)

    by_columns(y_ref.shape[1], body)


def third_kernel(third_ref, from_left_ref, from_right_ref, right_ref, left_ref):
    tok = right_ref.shape[0]
    half = tok // 2

    def body(cols):
        from_left = from_left_ref[:, cols].astype(F32)
        from_right = from_right_ref[:, cols].astype(F32)
        right_ref[:half, cols] = (third_ref[tok : tok + half, cols] + from_left).astype(BF16)
        right_ref[half:, cols] = third_ref[tok + half :, cols].astype(BF16)
        left_ref[:half, cols] = third_ref[:half, cols].astype(BF16)
        left_ref[half:, cols] = (third_ref[half:tok, cols] + from_right).astype(BF16)

    by_columns(right_ref.shape[1], body)


def second_kernel(
    mix, y_ref, from_left, from_right, right_ref, left_ref, mix_ref, from_left_ref, from_right_ref, sem
):
    tok = right_ref.shape[0]
    copies = [
        pltpu.make_async_copy(
            mix.at[n, pl.ds(3 * tok, 2 * tok), :], mix_ref.at[n], sem.at[n]
        )
        for n in range(2)
    ]
    copies.append(pltpu.make_async_copy(from_left, from_left_ref, sem.at[2]))
    copies.append(pltpu.make_async_copy(from_right, from_right_ref, sem.at[3]))
    for copy in copies:
        copy.start()
    for copy in copies:
        copy.wait()

    def body(cols):
        mixed = weighted(mix_ref, 0, 2 * tok, y_ref[:, cols])
        left_ref[:, cols] = (mixed[:tok] + from_right_ref[:, cols].astype(F32)).astype(BF16)
        right_ref[:, cols] = (mixed[tok:] + from_left_ref[:, cols].astype(F32)).astype(BF16)

    by_columns(y_ref.shape[1], body)


def first_kernel(mix_ref, y_ref, resid_ref, own_ref, base_ref, first_ref):
    tok = resid_ref.shape[0]

    def body(cols):
        mixed = weighted(mix_ref, 0, 3 * tok, y_ref[:, cols])
        base_ref[:, cols] = mixed[:tok] + own_ref[:, cols] + resid_ref[:, cols].astype(F32)
        first_ref[:, cols] = mixed[tok:]

    by_columns(y_ref.shape[1], body)


def add_kernel(first_ref, from_left_ref, from_right_ref, right_ref, left_ref):
    tok = right_ref.shape[0]
    left_ref[...] = (first_ref[:tok] + from_right_ref[...].astype(F32)).astype(BF16)
    right_ref[...] = (first_ref[tok:] + from_left_ref[...].astype(F32)).astype(BF16)


def last_kernel(base_ref, from_left_ref, from_right_ref, out_ref):
    total = base_ref[...] + from_left_ref[...].astype(F32) + from_right_ref[...].astype(F32)
    out_ref[...] = total.astype(BF16)


def ring(block, pools):
    right = [(k, (k + 1) % pools) for k in range(pools)]
    left = [(k, (k - 1) % pools) for k in range(pools)]
    pieces = [block]
    from_left = from_right = block
    for _ in range(1, pools // 2):
        from_left = lax.ppermute(from_left, "pool", right)
        from_right = lax.ppermute(from_right, "pool", left)
        pieces += [from_left, from_right]
    half = block.shape[0] // 2
    pieces += [
        lax.ppermute(from_left[:half], "pool", right),
        lax.ppermute(from_right[half:], "pool", left),
    ]
    return pieces


def shards(
    residual,
    queries,
    fresh_kv,
    pool_cache,
    hit_blocks,
    norm_gain,
    route_ids,
    route_logits,
    w_gate,
    w_up,
    w_down,
):
    pools = lax.axis_size("pool")
    plane = lax.axis_size("xy")
    rank = lax.axis_index("pool").astype(jnp.int32)[None]
    _, tok, model = queries.shape
    held, block, width = pool_cache.shape
    hits = hit_blocks.shape[1]
    top = route_ids.shape[2]
    half = w_gate.shape[2]
    shape = jax.ShapeDtypeStruct

    swap = [(0, 1), (1, 0)]
    own = (w_gate[0], w_up[0], w_down[0])
    peer = tuple(lax.ppermute(w, "core", swap) for w in own)

    (packed,) = held_call(
        gather_kernel,
        "gather_block",
        [shape((tok, 2 * width + META), BF16)],
        [
            rank,
            hit_blocks,
            (pool_cache,),
            Fetched((fresh_kv[0],)),
            Fetched((route_ids[0].T,)),
            Fetched((route_logits[0].T,)),
        ],
        scalars=2,
        near=(0,),
        scratch=[pltpu.SemaphoreType.DMA((HOT,))],
    )
    pieces = ring(packed, pools)

    stack = 4
    keys = hits * block + pools * tok
    attended, resid, normed, meta = held_call(
        lambda *refs: attend_kernel(*refs, pools=pools, held=held),
        "attend",
        [shape((tok, model), BF16)] * 3 + [shape((pools * tok, META), BF16)],
        [
            rank,
            hit_blocks,
            Fetched((norm_gain[None],)),
            Fetched((queries[0],)),
            Fetched((residual[0],)),
            *pieces,
        ],
        scalars=2,
        near=(2, 3),
        scratch=[
            pltpu.VMEM((pools * tok, 2 * width + META), BF16),
            pltpu.VMEM((keys, width), BF16),
            pltpu.VMEM((stack * tok, keys), F32),
        ],
    )

    near_slots, far_slots = plane * NEAR_SLOTS, plane * FAR_SLOTS
    near_rows, far_rows = NEAR * tok, (pools - NEAR + 1) * tok
    take_near, take_far, mix_near, mix_far = held_call(
        lambda *refs: route_kernel(*refs, pools=pools, top=top),
        "route",
        [
            shape((near_slots, near_rows), BF16),
            shape((far_slots, far_rows), BF16),
            shape((2, near_rows, near_slots), BF16),
            shape((2, far_rows, far_slots), BF16),
        ],
        [rank, meta],
        scalars=1,
        near=(0,),
        scratch=[pltpu.VMEM((near_rows, near_slots), F32)],
    )

    def pack(take, parts_in, name):
        slots, rows = (take[0] if isinstance(take, tuple) else take).shape
        parts = model // COLS
        (out,) = held_call(
            pack_kernel,
            name,
            [shape((slots, model), BF16)],
            [take, *parts_in],
            far=(0,),
            scratch=[
                pltpu.VMEM((rows, COLS), BF16),
                pltpu.VMEM((parts, slots, COLS), BF16),
                pltpu.SemaphoreType.DMA((parts,)),
            ],
            limit=32,
        )
        return out

    def exchange(x):
        slots = x.shape[0]
        x = x.reshape(plane, slots // plane, model)
        return lax.all_to_all(x, "xy", split_axis=0, concat_axis=0, tiled=True).reshape(
            slots, model
        )

    def expert(x, name):
        slots = x.shape[0]
        parts, ends = 4, 4
        dma = pltpu.SemaphoreType.DMA
        (out,) = held_call(
            expert_kernel,
            name,
            [shape((slots, model), BF16)],
            [(x,)] + [(w,) for pair in zip(own, peer) for w in pair],
            far=(0,),
            scratch=[
                pltpu.VMEM((slots, model), BF16),
                pltpu.VMEM((2, model, 2 * half), BF16),
                pltpu.VMEM((ends, 2 * half, model // ends), BF16),
                pltpu.VMEM((2, slots, 2 * half), F32),
                pltpu.VMEM((slots, 2 * half), BF16),
                pltpu.VMEM((ends, slots, model // ends), BF16),
                dma((parts,)),
                dma((2, parts, 2)),
                dma((ends, 2)),
                dma((ends,)),
            ],
            limit=48,
        )
        return out

    right = [(k, (k + 1) % pools) for k in range(pools)]
    left = [(k, (k - 1) % pools) for k in range(pools)]
    send = lambda r, l: (lax.ppermute(r, "pool", right), lax.ppermute(l, "pool", left))
    tie = lax.optimization_barrier

    once = send(normed, normed)
    once, take_near, peer = tie((once, take_near, peer))
    twice = send(*once)
    sent_near = pack(take_near, [normed, *once, *twice], "pack_near")
    thrice = send(*twice)
    fourth = send(thrice[0][: tok // 2], thrice[1][tok // 2 :])
    sent_far = pack(Fetched((take_far,)), [Fetched((normed,)), *thrice, *fourth], "pack_far")
    got_near = exchange(sent_near)
    got_near, sent_far = tie((got_near, sent_far))
    got_far = exchange(sent_far)
    out_near = expert(got_near, "expert_near")
    got_far, out_near = tie((got_far, out_near))
    out_far = expert(got_far, "expert_far")
    back_far = exchange(out_far)
    out_near, back_far = tie((out_near, back_far))
    back_near = exchange(out_near)

    row, pair = (tok, model), (2 * tok, model)
    own_far, third, *moving = held_call(
        far_kernel,
        "mix_far",
        [shape(row, F32), shape(pair, F32)] + [shape((tok // 2, model), BF16)] * 2,
        [Fetched((mix_far,)), Fetched((back_far,))],
        near=(1, 2, 3),
    )
    moving = held_call(
        third_kernel,
        "add_third",
        [shape(row, BF16)] * 2,
        [third, *send(*moving)],
        near=(0, 1),
        limit=16,
    )
    moving = held_call(
        second_kernel,
        "mix_second",
        [shape(row, BF16)] * 2,
        [in_hbm(mix_near), back_near, *[in_hbm(m) for m in send(*moving)]],
        near=(0, 1),
        scratch=[
            pltpu.VMEM((2, 2 * tok, near_slots), BF16),
            pltpu.VMEM(row, BF16),
            pltpu.VMEM(row, BF16),
            pltpu.SemaphoreType.DMA((4,)),
        ],
        limit=24,
    )
    moving = send(*moving)
    base, first = held_call(
        first_kernel,
        "mix_first",
        [shape(row, F32), shape(pair, F32)],
        [Fetched((mix_near,)), back_near, Fetched((resid,)), Fetched((own_far,))],
        near=(0, 1),
        limit=24,
    )
    moving = held_call(
        add_kernel, "add_first", [shape(row, BF16)] * 2, [first, *moving], near=(0, 1), limit=16
    )
    (layer_out,) = held_call(
        last_kernel, "add_last", [shape(row, BF16)], [base, *send(*moving)], limit=16
    )
    return (attended[None], layer_out[None])


def solution(mesh):
    pools, experts = mesh.devices.shape
    fine = Mesh(mesh.devices.reshape(pools, experts // 2, 2), ("pool", "xy", "core"))
    ex = ("xy", "core")
    tokens = P(ex, "pool", None)
    slab = P(("pool", "xy", "core"), None, None)
    placed = (
        tokens,
        tokens,
        tokens,
        P("pool", None, None),
        P(ex, None),
        P(),
        tokens,
        tokens,
        slab,
        slab,
        slab,
    )
    return jax.shard_map(
        shards, mesh=fine, in_specs=placed, out_specs=(tokens, tokens), check_vma=False
    )
```

```python
import jax
import jax.numpy as jnp
from jax import lax
from jax.experimental import pallas as pl
from jax.experimental.pallas import tpu as pltpu
from jax.sharding import Mesh, PartitionSpec as P

HD = 128
HOT = 4
MOST = 5
META = 128
FIRST = [(0, 0), (0, 1), (0, 2), (0, 3), (1, 0), (1, 1), (2, 0), (2, 1)]
MID = [(p, k) for p in (1, 2) for k in (2, 3, 4)] + [(p, k) for p in (3, 4) for k in range(MOST)]
FAR = [(0, 4)] + [(p, k) for p in (5, 6, 7) for k in range(MOST)]
TAKE_NEAR, TAKE_FAR = (FIRST + MID, 0, 5), (FAR, 4, 4)
MIX_FIRST, MIX_MID, MIX_FAR = (FIRST, 0, 3), (MID, 1, 4), (FAR, 4, 4)
MASKED = -1e30
EPSILON = 1e-06
F32 = jnp.float32
BF16 = jnp.bfloat16
COLS = 1024

SMEM = pl.BlockSpec(memory_space=pltpu.SMEM)
VMEM = pl.BlockSpec(memory_space=pltpu.VMEM)
ANY = pl.BlockSpec(memory_space=pl.ANY)


class Fetched(tuple):
    pass


def in_hbm(x):
    return (pltpu.with_memory_space_constraint(x, pltpu.HBM),)


def held_call(kernel, name, outs, args, scalars=0, near=(), far=(), scratch=(), limit=56):
    given = list(args[:scalars])
    specs = [SMEM] * scalars
    for arg in args[scalars:]:
        if isinstance(arg, tuple):
            given.append(arg[0])
            specs.append(VMEM if isinstance(arg, Fetched) else ANY)
        else:
            given.append(pltpu.with_memory_space_constraint(arg, pltpu.VMEM))
            specs.append(VMEM)
    return pl.pallas_call(
        kernel,
        in_specs=specs,
        out_specs=[ANY if n in far else VMEM for n in range(len(outs))],
        out_shape=[
            pltpu.VMEM(o.shape, o.dtype) if n in near else o for n, o in enumerate(outs)
        ],
        scratch_shapes=list(scratch),
        compiler_params=pltpu.CompilerParams(vmem_limit_bytes=limit * 1024 * 1024),
        name=name,
    )(*given)


def gather_kernel(rank_ref, hit_ref, cache_ref, fresh_ref, ids_ref, logit_ref, out_ref, sem):
    rank = rank_ref[0]
    held, block, width = cache_ref.shape
    count = jnp.int32(0)
    local = [jnp.int32(0)] * HOT
    for i in range(hit_ref.shape[1]):
        hit = hit_ref[0, i]
        mine = lax.div(hit, held) == rank
        for slot in range(HOT):
            local[slot] = jnp.where(mine & (count == slot), lax.rem(hit, held), local[slot])
        count = count + mine.astype(jnp.int32)
    copies = [
        pltpu.make_async_copy(
            cache_ref.at[local[slot]],
            out_ref.at[slot * block : (slot + 1) * block, :width],
            sem.at[slot],
        )
        for slot in range(HOT)
    ]
    for copy in copies:
        copy.start()
    out_ref[:, width : 2 * width] = fresh_ref[...]
    ids = ids_ref[...].astype(F32).T
    logits = logit_ref[...].T
    grown = jnp.exp(logits - jnp.max(logits, axis=-1, keepdims=True))
    weight = grown / jnp.sum(grown, axis=-1, keepdims=True)
    high = weight.astype(BF16).astype(F32)
    low = weight - high
    tok, top = ids.shape
    lane = lax.broadcasted_iota(jnp.int32, (tok, META), 1)
    meta = jnp.zeros((tok, META), F32)
    for part, values in enumerate((ids, high, low)):
        for j in range(top):
            meta = jnp.where(lane == part * top + j, values[:, j : j + 1], meta)
    out_ref[:, 2 * width :] = meta.astype(BF16)
    for copy in copies:
        copy.wait()


def place_ring(rank, pools, tok, pieces, store):
    store(rank * tok, pieces[0][...])
    half = pools // 2
    for s in range(1, half):
        store(lax.rem(rank + pools - s, pools) * tok, pieces[2 * s - 1][...])
        store(lax.rem(rank + s, pools) * tok, pieces[2 * s][...])
    far = lax.rem(rank + half, pools) * tok
    store(far, pieces[2 * half - 1][...])
    store(far + tok // 2, pieces[2 * half][...])


def attend_kernel(rank_ref, hit_ref, gain_ref, query_ref, residual_ref, *refs, pools, held):
    pieces = refs[: pools + 1]
    attended_ref, resid_ref, normed_ref, meta_ref, part_ref, kv_ref, bias_ref = refs[pools + 1 :]
    rank = rank_ref[0]
    tok, model = query_ref.shape
    hits = hit_ref.shape[1]
    width = kv_ref.shape[1]
    block = tok // HOT

    def store(row, value):
        part_ref[pl.ds(pl.multiple_of(row, tok // 2), value.shape[0]), :] = value

    place_ring(rank, pools, tok, pieces, store)
    meta_ref[...] = part_ref[:, 2 * width :]
    owners = [lax.div(hit_ref[0, i], held) for i in range(hits)]
    for i in range(hits):
        slot = jnp.int32(0)
        for earlier in range(i):
            slot = slot + (owners[earlier] == owners[i]).astype(jnp.int32)
        row = pl.multiple_of(owners[i] * tok + jnp.minimum(slot, HOT - 1) * block, block)
        kv_ref[i * block : (i + 1) * block, :] = part_ref[pl.ds(row, block), :width]
    prefix = hits * block
    kv_ref[prefix:, :] = part_ref[:, width : 2 * width]
    heads_kv = width // (2 * HD)
    group = model // (heads_kv * HD)
    rows, keys = bias_ref.shape
    stack = rows // tok
    col = lax.broadcasted_iota(jnp.int32, (rows, keys), 1)
    position = lax.rem(lax.broadcasted_iota(jnp.int32, (rows, keys), 0), tok) + rank * tok
    bias_ref[...] = jnp.where(col - prefix <= position, 0.0, MASKED)

    def some_heads(n, squares):
        lane = lambda at: pl.ds(pl.multiple_of(at * HD, HD), HD)
        first = n * stack
        g = lax.div(first, group)
        query = jnp.concatenate([query_ref[:, lane(first + h)] for h in range(stack)], axis=0)
        scores = lax.dot_general(
            query, kv_ref[:, lane(g)], (((1,), (1,)), ((), ())), preferred_element_type=F32
        )
        scores = scores * HD ** (-0.5) + bias_ref[...]
        weights = jnp.exp(scores - jnp.max(scores, axis=-1, keepdims=True))
        row_sum = jnp.sum(weights, axis=-1, keepdims=True)
        mixed = jnp.dot(
            weights.astype(BF16), kv_ref[:, lane(heads_kv + g)], preferred_element_type=F32
        )
        mixed = (mixed / row_sum).astype(BF16)
        for h in range(stack):
            part = mixed[h * tok : (h + 1) * tok]
            attended_ref[:, lane(first + h)] = part
            wide = residual_ref[:, lane(first + h)].astype(F32) + part.astype(F32)
            resid = wide.astype(BF16)
            resid_ref[:, lane(first + h)] = resid
            wide = resid.astype(F32)
            squares = squares + wide * wide
        return squares

    squares = lax.fori_loop(
        0,
        model // (2 * stack * HD),
        lambda n, squares: some_heads(2 * n + 1, some_heads(2 * n, squares)),
        jnp.zeros((tok, HD), F32),
    )
    inv_rms = lax.rsqrt(jnp.sum(squares, axis=-1, keepdims=True) / model + EPSILON)
    normed_ref[...] = (resid_ref[...].astype(F32) * inv_rms * gain_ref[...]).astype(BF16)


def offset_of(piece):
    far = lax.div(piece + 1, 2)
    return jnp.where((lax.rem(piece, 2) == 1) & (piece < 7), -far, far)


def route_kernel(rank_ref, meta_ref, *refs, pools, top):
    takes, mixes, named_ref = refs[:2], refs[2:5], refs[5]
    tok = meta_ref.shape[0] // pools
    rank = rank_ref[0]
    plane = takes[0].shape[0] // len(TAKE_NEAR[0])
    before = (
        lax.broadcasted_iota(jnp.int32, (tok, tok), 1)
        < lax.broadcasted_iota(jnp.int32, (tok, tok), 0)
    ).astype(BF16)

    def fill(table, take_ref, mix_ref):
        part, first, count = table
        per = len(part)
        slots = plane * per
        slot = lax.broadcasted_iota(jnp.int32, (1, slots), 1)
        inner = lax.rem(slot, per)
        expert = (lax.div(slot, per) + rank * plane).astype(F32)
        of_piece = jnp.zeros((1, slots), jnp.int32)
        place = jnp.zeros((1, slots), F32)
        for n, (p, k) in enumerate(part):
            of_piece = jnp.where(inner == n, p, of_piece)
            place = jnp.where(inner == n, float(k), place)

        def one_piece(at, carry):
            piece = at + first
            if table in (TAKE_FAR, MIX_FAR):
                piece = jnp.where(at == 0, 0, piece)
            row = lax.rem(rank + pools + offset_of(piece), pools) * tok
            meta = meta_ref[pl.ds(pl.multiple_of(row, tok), tok), :].astype(F32)
            named = jnp.zeros((tok, slots), F32)
            high = jnp.zeros((tok, slots), F32)
            low = jnp.zeros((tok, slots), F32)
            for j in range(top):
                same = meta[:, j : j + 1] == expert
                named = jnp.where(same, 1.0, named)
                if mix_ref is not None:
                    high = jnp.where(same, meta[:, top + j : top + j + 1], high)
                    low = jnp.where(same, meta[:, 2 * top + j : 2 * top + j + 1], low)
            ahead = jnp.dot(before, named.astype(BF16), preferred_element_type=F32)
            chosen = (named > 0.5) & (ahead == jnp.where(of_piece == piece, place, -1.0))
            here = pl.ds(pl.multiple_of(at * tok, tok), tok)
            if take_ref is not None:
                named_ref[here, :slots] = jnp.where(chosen, 1.0, 0.0)
            if mix_ref is not None:
                mix_ref[0, here, :] = jnp.where(chosen, high, 0.0).astype(BF16)
                mix_ref[1, here, :] = jnp.where(chosen, low, 0.0).astype(BF16)
            return carry

        lax.fori_loop(0, count, one_piece, 0)
        if take_ref is not None:
            take_ref[...] = named_ref[: count * tok, :slots].T.astype(BF16)

    fill(TAKE_NEAR, takes[0], None)
    fill(TAKE_FAR, takes[1], mixes[2])
    fill(MIX_FIRST, None, mixes[0])
    fill(MIX_MID, None, mixes[1])


def by_columns(width, body):
    def step(n, carry):
        body(pl.ds(pl.multiple_of(n * COLS, COLS), COLS))
        return carry

    lax.fori_loop(0, width // COLS, step, 0)


def pack_kernel(take_ref, *refs):
    pieces, (out_ref, rows_ref, packed_ref, sem) = refs[:-4], refs[-4:]
    wide = packed_ref.shape[2]

    def leave(n):
        cols = pl.ds(pl.multiple_of(n * wide, wide), wide)
        return pltpu.make_async_copy(packed_ref.at[n], out_ref.at[:, cols], sem.at[n])

    def step(n, carry):
        cols = pl.ds(pl.multiple_of(n * wide, wide), wide)
        at = 0
        for piece in pieces:
            rows_ref[at : at + piece.shape[0], :] = piece[:, cols]
            at += piece.shape[0]
        packed_ref[n] = jnp.dot(
            take_ref[...], rows_ref[...], preferred_element_type=F32
        ).astype(BF16)
        leave(n).start()
        return carry

    parts = sem.shape[0]
    lax.fori_loop(0, parts, step, 0)
    for n in range(parts):
        leave(n).wait()


def expert_kernel(x, g0, g1, u0, u1, d0, d1, *refs):
    outs = refs[:-10]
    x_ref, grow_ref, down_ref, sum_ref, hidden_ref, y_ref, x_sem, grow_sem, down_sem, out_sem = (
        refs[-10:]
    )
    half = g0.shape[1]
    parts = x_sem.shape[0]
    deep = x.shape[1] // parts
    ends = out_sem.shape[0]
    wide = x.shape[1] // ends

    def row_copy(n):
        cols = pl.ds(pl.multiple_of(n * deep, deep), deep)
        return pltpu.make_async_copy(x.at[:, cols], x_ref.at[:, cols], x_sem.at[n])

    def grow_copies(slab, n, gate, up):
        rows = pl.ds(pl.multiple_of(n * deep, deep), deep)
        return [
            pltpu.make_async_copy(
                w.at[rows, :],
                grow_ref.at[slab, rows, pl.ds(at * half, half)],
                grow_sem.at[slab, n, at],
            )
            for at, w in enumerate((gate, up))
        ]

    def down_copies(n):
        cols = pl.ds(pl.multiple_of(n * wide, wide), wide)
        return [
            pltpu.make_async_copy(
                w.at[:, cols], down_ref.at[n, pl.ds(at * half, half), :], down_sem.at[n, at]
            )
            for at, w in enumerate((d0, d1))
        ]

    def leave(n):
        cols = pl.ds(pl.multiple_of(n * wide, wide), wide)
        copies, at = [], 0
        for c, out in enumerate(outs):
            rows = out.shape[1]
            copies.append(
                pltpu.make_async_copy(
                    y_ref.at[n, :, pl.ds(at, rows), :], out.at[:, :, cols], out_sem.at[n, c]
                )
            )
            at += rows
        return copies

    for slab, (gate, up) in enumerate(((g0, u0), (g1, u1))):
        for n in range(parts):
            if slab == 0:
                row_copy(n).start()
            for copy in grow_copies(slab, n, gate, up):
                copy.start()
    for n in range(ends):
        for copy in down_copies(n):
            copy.start()

    def grow(step, carry):
        slab, n = lax.div(step, parts), lax.rem(step, parts)

        @pl.when(slab == 0)
        def _():
            row_copy(n).wait()

        for copy in grow_copies(slab, n, g0, u0):
            copy.wait()
        part = pl.ds(pl.multiple_of(n * deep, deep), deep)
        grown = jnp.dot(x_ref[:, part], grow_ref[slab, part, :], preferred_element_type=F32)
        sum_ref[slab] += grown
        return carry

    sum_ref[...] = jnp.zeros(sum_ref.shape, F32)
    lax.fori_loop(0, 2 * parts, grow, 0)
    for slab in range(2):
        gate, up = sum_ref[slab, :, :half], sum_ref[slab, :, half:]
        hidden = gate / (1.0 + jnp.exp(-gate)) * up
        hidden_ref[:, slab * half : (slab + 1) * half] = hidden.astype(BF16)

    def shrink(n, carry):
        for copy in down_copies(n):
            copy.wait()
        y = jnp.dot(hidden_ref[...], down_ref[n], preferred_element_type=F32)
        y_ref[n] = y.reshape(y_ref.shape[1:]).astype(BF16)
        for copy in leave(n):
            copy.start()
        return carry

    lax.fori_loop(0, ends, shrink, 0)
    for n in range(ends):
        for copy in leave(n):
            copy.wait()


def weighted(mix_ref, first, last, y):
    return jnp.dot(mix_ref[0, first:last, :], y, preferred_element_type=F32) + jnp.dot(
        mix_ref[1, first:last, :], y, preferred_element_type=F32
    )


def far_kernel(mix_ref, y_ref, own_ref, third_ref, right_ref, left_ref):
    tok = own_ref.shape[0]
    half = tok // 2

    def body(cols):
        mixed = weighted(mix_ref, 0, mix_ref.shape[1], y_ref[:, cols])
        own_ref[:, cols] = mixed[:tok]
        third_ref[:, cols] = mixed[tok : 3 * tok]
        right_ref[:, cols] = mixed[3 * tok : 3 * tok + half].astype(BF16)
        left_ref[:, cols] = mixed[3 * tok + half :].astype(BF16)

    by_columns(y_ref.shape[1], body)


def third_kernel(third_ref, from_left_ref, from_right_ref, right_ref, left_ref):
    tok = right_ref.shape[0]
    half = tok // 2

    def body(cols):
        from_left = from_left_ref[:, cols].astype(F32)
        from_right = from_right_ref[:, cols].astype(F32)
        right_ref[:half, cols] = (third_ref[tok : tok + half, cols] + from_left).astype(BF16)
        right_ref[half:, cols] = third_ref[tok + half :, cols].astype(BF16)
        left_ref[:half, cols] = third_ref[:half, cols].astype(BF16)
        left_ref[half:, cols] = (third_ref[half:tok, cols] + from_right).astype(BF16)

    by_columns(right_ref.shape[1], body)


def second_kernel(
    mix, y_ref, from_left, from_right, right_ref, left_ref, mix_ref, from_left_ref, from_right_ref, sem
):
    tok = right_ref.shape[0]
    copies = [
        pltpu.make_async_copy(
            mix.at[n, pl.ds(2 * tok, 2 * tok), :], mix_ref.at[n], sem.at[n]
        )
        for n in range(2)
    ]
    copies.append(pltpu.make_async_copy(from_left, from_left_ref, sem.at[2]))
    copies.append(pltpu.make_async_copy(from_right, from_right_ref, sem.at[3]))
    for copy in copies:
        copy.start()
    for copy in copies[:2]:
        copy.wait()

    def body(cols):
        mixed = weighted(mix_ref, 0, 2 * tok, y_ref[:, cols])

        @pl.when(cols.start == 0)
        def _():
            for copy in copies[2:]:
                copy.wait()

        left_ref[:, cols] = (mixed[:tok] + from_right_ref[:, cols].astype(F32)).astype(BF16)
        right_ref[:, cols] = (mixed[tok:] + from_left_ref[:, cols].astype(F32)).astype(BF16)

    by_columns(y_ref.shape[1], body)


def first_kernel(
    near_ref, near_y_ref, mix_ref, y_ref, resid_ref, own_ref, base_ref, first_ref
):
    tok = resid_ref.shape[0]

    def body(cols):
        near = weighted(near_ref, 0, 3 * tok, near_y_ref[:, cols])
        mixed = weighted(mix_ref, 0, 2 * tok, y_ref[:, cols])
        base_ref[:, cols] = near[:tok] + own_ref[:, cols] + resid_ref[:, cols].astype(F32)
        first_ref[:, cols] = near[tok:] + mixed

    by_columns(y_ref.shape[1], body)


def add_kernel(first_ref, from_left_ref, from_right_ref, right_ref, left_ref):
    tok = right_ref.shape[0]
    left_ref[...] = (first_ref[:tok] + from_right_ref[...].astype(F32)).astype(BF16)
    right_ref[...] = (first_ref[tok:] + from_left_ref[...].astype(F32)).astype(BF16)


def last_kernel(base_ref, from_left_ref, from_right_ref, out_ref):
    total = base_ref[...] + from_left_ref[...].astype(F32) + from_right_ref[...].astype(F32)
    out_ref[...] = total.astype(BF16)


def ring(block, pools):
    right = [(k, (k + 1) % pools) for k in range(pools)]
    left = [(k, (k - 1) % pools) for k in range(pools)]
    pieces = [block]
    from_left = from_right = block
    for _ in range(1, pools // 2):
        from_left = lax.ppermute(from_left, "pool", right)
        from_right = lax.ppermute(from_right, "pool", left)
        pieces += [from_left, from_right]
    half = block.shape[0] // 2
    pieces += [
        lax.ppermute(from_left[:half], "pool", right),
        lax.ppermute(from_right[half:], "pool", left),
    ]
    return pieces


def shards(
    residual,
    queries,
    fresh_kv,
    pool_cache,
    hit_blocks,
    norm_gain,
    route_ids,
    route_logits,
    w_gate,
    w_up,
    w_down,
):
    pools = lax.axis_size("pool")
    plane = lax.axis_size("xy")
    rank = lax.axis_index("pool").astype(jnp.int32)[None]
    _, tok, model = queries.shape
    held, block, width = pool_cache.shape
    hits = hit_blocks.shape[1]
    top = route_ids.shape[2]
    half = w_gate.shape[2]
    shape = jax.ShapeDtypeStruct

    swap = [(0, 1), (1, 0)]
    own = (w_gate[0], w_up[0], w_down[0])
    peer = tuple(lax.ppermute(w, "core", swap) for w in own)

    (packed,) = held_call(
        gather_kernel,
        "gather_block",
        [shape((tok, 2 * width + META), BF16)],
        [
            rank,
            hit_blocks,
            (pool_cache,),
            Fetched((fresh_kv[0],)),
            Fetched((route_ids[0].T,)),
            Fetched((route_logits[0].T,)),
        ],
        scalars=2,
        near=(0,),
        scratch=[pltpu.SemaphoreType.DMA((HOT,))],
    )
    pieces = ring(packed, pools)

    stack = 4
    keys = hits * block + pools * tok
    attended, resid, normed, meta = held_call(
        lambda *refs: attend_kernel(*refs, pools=pools, held=held),
        "attend",
        [shape((tok, model), BF16)] * 3 + [shape((pools * tok, META), BF16)],
        [
            rank,
            hit_blocks,
            Fetched((norm_gain[None],)),
            Fetched((queries[0],)),
            Fetched((residual[0],)),
            *pieces,
        ],
        scalars=2,
        near=(2, 3),
        scratch=[
            pltpu.VMEM((pools * tok, 2 * width + META), BF16),
            pltpu.VMEM((keys, width), BF16),
            pltpu.VMEM((stack * tok, keys), F32),
        ],
    )

    def size(table):
        return plane * len(table[0]), table[2] * tok

    mixing = (MIX_FIRST, MIX_MID, MIX_FAR)
    take_near, take_far, mix_first, mix_mid, mix_far = held_call(
        lambda *refs: route_kernel(*refs, pools=pools, top=top),
        "route",
        [shape(size(t), BF16) for t in (TAKE_NEAR, TAKE_FAR)]
        + [shape((2,) + size(t)[::-1], BF16) for t in mixing],
        [rank, meta],
        scalars=1,
        near=(0,),
        scratch=[pltpu.VMEM(size(TAKE_NEAR)[::-1], F32)],
    )

    def pack(take, parts_in, name):
        slots, rows = (take[0] if isinstance(take, tuple) else take).shape
        parts = model // COLS
        (out,) = held_call(
            pack_kernel,
            name,
            [shape((slots, model), BF16)],
            [take, *parts_in],
            far=(0,),
            scratch=[
                pltpu.VMEM((rows, COLS), BF16),
                pltpu.VMEM((parts, slots, COLS), BF16),
                pltpu.SemaphoreType.DMA((parts,)),
            ],
            limit=32,
        )
        return out

    def exchange(x):
        x = x.reshape(plane, -1, model)
        return lax.all_to_all(x, "xy", split_axis=0, concat_axis=0, tiled=True).reshape(
            -1, model
        )

    def expert(x, splits, name):
        slots = x.shape[0]
        parts, ends = 4, 4
        dma = pltpu.SemaphoreType.DMA
        return held_call(
            expert_kernel,
            name,
            [shape((plane, rows, model), BF16) for rows in splits],
            [(x,)] + [(w,) for pair in zip(own, peer) for w in pair],
            far=range(len(splits)),
            scratch=[
                pltpu.VMEM((slots, model), BF16),
                pltpu.VMEM((2, model, 2 * half), BF16),
                pltpu.VMEM((ends, 2 * half, model // ends), BF16),
                pltpu.VMEM((2, slots, 2 * half), F32),
                pltpu.VMEM((slots, 2 * half), BF16),
                pltpu.VMEM((ends, plane, slots // plane, model // ends), BF16),
                dma((parts,)),
                dma((2, parts, 2)),
                dma((ends, 2)),
                dma((ends, len(splits))),
            ],
            limit=48,
        )

    right = [(k, (k + 1) % pools) for k in range(pools)]
    left = [(k, (k - 1) % pools) for k in range(pools)]
    send = lambda r, l: (lax.ppermute(r, "pool", right), lax.ppermute(l, "pool", left))
    tie = lax.optimization_barrier

    once = send(normed, normed)
    once, take_near, peer = tie((once, take_near, peer))
    twice = send(*once)
    sent_near = pack(take_near, [normed, *once, *twice], "pack_near")
    thrice = send(*twice)
    fourth = send(thrice[0][: tok // 2], thrice[1][tok // 2 :])
    sent_far = pack(Fetched((take_far,)), [Fetched((normed,)), *thrice, *fourth], "pack_far")
    got_near = exchange(sent_near)
    got_near, sent_far = tie((got_near, sent_far))
    got_far = exchange(sent_far)
    out_first, out_mid = expert(got_near, (len(FIRST), len(MID)), "expert_near")
    got_far, out_first, out_mid = tie((got_far, out_first, out_mid))
    (out_far,) = expert(got_far, (len(FAR),), "expert_far")
    back_far = exchange(out_far)
    out_mid, back_far = tie((out_mid, back_far))
    back_mid = exchange(out_mid)
    out_first, back_mid = tie((out_first, back_mid))
    back_first = exchange(out_first)

    row, pair = (tok, model), (2 * tok, model)
    own_far, third, *moving = held_call(
        far_kernel,
        "mix_far",
        [shape(row, F32), shape(pair, F32)] + [shape((tok // 2, model), BF16)] * 2,
        [Fetched((mix_far,)), Fetched((back_far,))],
        near=(1, 2, 3),
    )
    moving = held_call(
        third_kernel,
        "add_third",
        [shape(row, BF16)] * 2,
        [third, *send(*moving)],
        near=(0, 1),
        limit=16,
    )
    moving = held_call(
        second_kernel,
        "mix_second",
        [shape(row, BF16)] * 2,
        [in_hbm(mix_mid), back_mid, *[in_hbm(m) for m in send(*moving)]],
        near=(0, 1),
        scratch=[
            pltpu.VMEM((2, 2 * tok, plane * len(MID)), BF16),
            pltpu.VMEM(row, BF16),
            pltpu.VMEM(row, BF16),
            pltpu.SemaphoreType.DMA((4,)),
        ],
        limit=24,
    )
    moving = send(*moving)
    base, first = held_call(
        first_kernel,
        "mix_first",
        [shape(row, F32), shape(pair, F32)],
        [
            Fetched((mix_first,)),
            Fetched((back_first,)),
            Fetched((mix_mid,)),
            back_mid,
            Fetched((resid,)),
            Fetched((own_far,)),
        ],
        near=(0, 1),
        limit=24,
    )
    moving = held_call(
        add_kernel, "add_first", [shape(row, BF16)] * 2, [first, *moving], near=(0, 1), limit=16
    )
    (layer_out,) = held_call(
        last_kernel, "add_last", [shape(row, BF16)], [base, *send(*moving)], limit=16
    )
    return (attended[None], layer_out[None])


def solution(mesh):
    pools, experts = mesh.devices.shape
    fine = Mesh(mesh.devices.reshape(pools, experts // 2, 2), ("pool", "xy", "core"))
    ex = ("xy", "core")
    tokens = P(ex, "pool", None)
    slab = P(("pool", "xy", "core"), None, None)
    placed = (
        tokens,
        tokens,
        tokens,
        P("pool", None, None),
        P(ex, None),
        P(),
        tokens,
        tokens,
        slab,
        slab,
        slab,
    )
    return jax.shard_map(
        shards, mesh=fine, in_specs=placed, out_specs=(tokens, tokens), check_vma=False
    )
```

```python
import jax
import jax.numpy as jnp
from jax import lax
from jax.experimental import pallas as pl
from jax.experimental.pallas import tpu as pltpu
from jax.sharding import Mesh, PartitionSpec as P

HD = 128
HOT = 4
MOST = 5
META = 128
FIRST = [(0, 0), (0, 1), (0, 2), (0, 3), (1, 0), (1, 1), (2, 0), (2, 1)]
MID = [(p, k) for p in (1, 2) for k in (2, 3, 4)] + [(p, k) for p in (3, 4) for k in range(MOST)]
FAR = [(0, 4)] + [(p, k) for p in (5, 6, 7) for k in range(MOST)]
TAKE_NEAR, TAKE_FAR = (FIRST + MID, 0, 5), (FAR, 4, 4)
MIX_FIRST, MIX_MID, MIX_FAR = (FIRST, 0, 3), (MID, 1, 4), (FAR, 4, 4)
MASKED = -1e30
LOG2E = 1.4426950408889634
EPSILON = 1e-06
F32 = jnp.float32
BF16 = jnp.bfloat16
COLS = 1024

SMEM = pl.BlockSpec(memory_space=pltpu.SMEM)
VMEM = pl.BlockSpec(memory_space=pltpu.VMEM)
ANY = pl.BlockSpec(memory_space=pl.ANY)


class Fetched(tuple):
    pass


def in_hbm(x):
    return (pltpu.with_memory_space_constraint(x, pltpu.HBM),)


def held_call(kernel, name, outs, args, scalars=0, near=(), far=(), scratch=(), limit=56):
    given = list(args[:scalars])
    specs = [SMEM] * scalars
    for arg in args[scalars:]:
        if isinstance(arg, tuple):
            given.append(arg[0])
            specs.append(VMEM if isinstance(arg, Fetched) else ANY)
        else:
            given.append(pltpu.with_memory_space_constraint(arg, pltpu.VMEM))
            specs.append(VMEM)
    return pl.pallas_call(
        kernel,
        in_specs=specs,
        out_specs=[ANY if n in far else VMEM for n in range(len(outs))],
        out_shape=[
            pltpu.VMEM(o.shape, o.dtype) if n in near else o for n, o in enumerate(outs)
        ],
        scratch_shapes=list(scratch),
        compiler_params=pltpu.CompilerParams(vmem_limit_bytes=limit * 1024 * 1024),
        name=name,
    )(*given)


def gather_kernel(rank_ref, hit_ref, cache_ref, fresh_ref, ids_ref, logit_ref, out_ref, sem):
    rank = rank_ref[0]
    held, block, width = cache_ref.shape
    count = jnp.int32(0)
    local = [jnp.int32(0)] * HOT
    for i in range(hit_ref.shape[1]):
        hit = hit_ref[0, i]
        mine = lax.div(hit, held) == rank
        for slot in range(HOT):
            local[slot] = jnp.where(mine & (count == slot), lax.rem(hit, held), local[slot])
        count = count + mine.astype(jnp.int32)
    copies = [
        pltpu.make_async_copy(
            cache_ref.at[local[slot]],
            out_ref.at[slot * block : (slot + 1) * block, :width],
            sem.at[slot],
        )
        for slot in range(HOT)
    ]
    for copy in copies:
        copy.start()
    out_ref[:, width : 2 * width] = fresh_ref[...]
    ids = ids_ref[...].astype(F32).T
    logits = logit_ref[...].T
    grown = jnp.exp(logits - jnp.max(logits, axis=-1, keepdims=True))
    weight = grown / jnp.sum(grown, axis=-1, keepdims=True)
    high = weight.astype(BF16).astype(F32)
    low = weight - high
    tok, top = ids.shape
    lane = lax.broadcasted_iota(jnp.int32, (tok, META), 1)
    meta = jnp.zeros((tok, META), F32)
    for part, values in enumerate((ids, high, low)):
        for j in range(top):
            meta = jnp.where(lane == part * top + j, values[:, j : j + 1], meta)
    out_ref[:, 2 * width :] = meta.astype(BF16)
    for copy in copies:
        copy.wait()


def place_ring(rank, pools, tok, pieces, store):
    store(rank * tok, pieces[0][...])
    half = pools // 2
    for s in range(1, half):
        store(lax.rem(rank + pools - s, pools) * tok, pieces[2 * s - 1][...])
        store(lax.rem(rank + s, pools) * tok, pieces[2 * s][...])
    far = lax.rem(rank + half, pools) * tok
    store(far, pieces[2 * half - 1][...])
    store(far + tok // 2, pieces[2 * half][...])


def attend_kernel(rank_ref, hit_ref, gain_ref, query_ref, residual_ref, *refs, pools, held):
    pieces = refs[: pools + 1]
    attended_ref, resid_ref, normed_ref, meta_ref, part_ref, kv_ref, bias_ref = refs[pools + 1 :]
    rank = rank_ref[0]
    tok, model = query_ref.shape
    hits = hit_ref.shape[1]
    width = kv_ref.shape[1]
    block = tok // HOT

    def store(row, value):
        part_ref[pl.ds(pl.multiple_of(row, tok // 2), value.shape[0]), :] = value

    place_ring(rank, pools, tok, pieces, store)
    meta_ref[...] = part_ref[:, 2 * width :]
    owners = [lax.div(hit_ref[0, i], held) for i in range(hits)]
    for i in range(hits):
        slot = jnp.int32(0)
        for earlier in range(i):
            slot = slot + (owners[earlier] == owners[i]).astype(jnp.int32)
        row = pl.multiple_of(owners[i] * tok + jnp.minimum(slot, HOT - 1) * block, block)
        kv_ref[i * block : (i + 1) * block, :] = part_ref[pl.ds(row, block), :width]
    prefix = hits * block
    kv_ref[prefix:, :] = part_ref[:, width : 2 * width]
    heads_kv = width // (2 * HD)
    group = model // (heads_kv * HD)
    rows, keys = bias_ref.shape
    stack = rows // tok
    col = lax.broadcasted_iota(jnp.int32, (rows, keys), 1)
    position = lax.rem(lax.broadcasted_iota(jnp.int32, (rows, keys), 0), tok) + rank * tok
    bias_ref[...] = jnp.where(col <= position, 0.0, MASKED)

    def some_heads(n, squares):
        lane = lambda at: pl.ds(pl.multiple_of(at * HD, HD), HD)
        first = n * stack
        g = lax.div(first, group)
        query = jnp.concatenate([query_ref[:, lane(first + h)] for h in range(stack)], axis=0)
        held_keys, new_keys = kv_ref[:prefix, lane(g)], kv_ref[prefix:, lane(g)]
        across = (((1,), (1,)), ((), ()))
        held_scores = lax.dot_general(query, held_keys, across, preferred_element_type=F32)
        new_scores = lax.dot_general(query, new_keys, across, preferred_element_type=F32)
        new_scores = new_scores + bias_ref[...]
        peak = jnp.maximum(
            jnp.max(held_scores, axis=-1, keepdims=True),
            jnp.max(new_scores, axis=-1, keepdims=True),
        )
        held_weights = jnp.exp2((held_scores - peak) * (HD ** (-0.5) * LOG2E))
        new_weights = jnp.exp2((new_scores - peak) * (HD ** (-0.5) * LOG2E))
        row_sum = jnp.sum(held_weights, axis=-1, keepdims=True) + jnp.sum(
            new_weights, axis=-1, keepdims=True
        )
        at = lane(heads_kv + g)
        mixed = jnp.dot(
            held_weights.astype(BF16), kv_ref[:prefix, at], preferred_element_type=F32
        ) + jnp.dot(new_weights.astype(BF16), kv_ref[prefix:, at], preferred_element_type=F32)
        mixed = (mixed / row_sum).astype(BF16)
        for h in range(stack):
            part = mixed[h * tok : (h + 1) * tok]
            attended_ref[:, lane(first + h)] = part
            wide = residual_ref[:, lane(first + h)].astype(F32) + part.astype(F32)
            resid = wide.astype(BF16)
            resid_ref[:, lane(first + h)] = resid
            wide = resid.astype(F32)
            squares = squares + wide * wide
        return squares

    squares = lax.fori_loop(
        0,
        model // (2 * stack * HD),
        lambda n, squares: some_heads(2 * n + 1, some_heads(2 * n, squares)),
        jnp.zeros((tok, HD), F32),
    )
    inv_rms = lax.rsqrt(jnp.sum(squares, axis=-1, keepdims=True) / model + EPSILON)
    normed_ref[...] = (resid_ref[...].astype(F32) * inv_rms * gain_ref[...]).astype(BF16)


def offset_of(piece):
    far = lax.div(piece + 1, 2)
    return jnp.where((lax.rem(piece, 2) == 1) & (piece < 7), -far, far)


def route_kernel(rank_ref, meta_ref, *refs, pools, top):
    takes, mixes, named_ref = refs[:2], refs[2:5], refs[5]
    tok = meta_ref.shape[0] // pools
    rank = rank_ref[0]
    plane = takes[0].shape[0] // len(TAKE_NEAR[0])
    before = (
        lax.broadcasted_iota(jnp.int32, (tok, tok), 1)
        < lax.broadcasted_iota(jnp.int32, (tok, tok), 0)
    ).astype(BF16)

    def fill(table, take_ref, mix_ref):
        part, first, count = table
        per = len(part)
        slots = plane * per
        slot = lax.broadcasted_iota(jnp.int32, (1, slots), 1)
        inner = lax.rem(slot, per)
        expert = (lax.div(slot, per) + rank * plane).astype(F32)
        of_piece = jnp.zeros((1, slots), jnp.int32)
        place = jnp.zeros((1, slots), F32)
        for n, (p, k) in enumerate(part):
            of_piece = jnp.where(inner == n, p, of_piece)
            place = jnp.where(inner == n, float(k), place)

        def one_piece(at, carry):
            piece = at + first
            if table in (TAKE_FAR, MIX_FAR):
                piece = jnp.where(at == 0, 0, piece)
            row = lax.rem(rank + pools + offset_of(piece), pools) * tok
            meta = meta_ref[pl.ds(pl.multiple_of(row, tok), tok), :].astype(F32)
            named = jnp.zeros((tok, slots), F32)
            high = jnp.zeros((tok, slots), F32)
            low = jnp.zeros((tok, slots), F32)
            for j in range(top):
                same = meta[:, j : j + 1] == expert
                named = jnp.where(same, 1.0, named)
                if mix_ref is not None:
                    high = jnp.where(same, meta[:, top + j : top + j + 1], high)
                    low = jnp.where(same, meta[:, 2 * top + j : 2 * top + j + 1], low)
            ahead = jnp.dot(before, named.astype(BF16), preferred_element_type=F32)
            chosen = (named > 0.5) & (ahead == jnp.where(of_piece == piece, place, -1.0))
            here = pl.ds(pl.multiple_of(at * tok, tok), tok)
            if take_ref is not None:
                named_ref[here, :slots] = jnp.where(chosen, 1.0, 0.0)
            if mix_ref is not None:
                mix_ref[0, here, :] = jnp.where(chosen, high, 0.0).astype(BF16)
                mix_ref[1, here, :] = jnp.where(chosen, low, 0.0).astype(BF16)
            return carry

        lax.fori_loop(0, count, one_piece, 0)
        if take_ref is not None:
            take_ref[...] = named_ref[: count * tok, :slots].T.astype(BF16)

    fill(TAKE_NEAR, takes[0], None)
    fill(TAKE_FAR, takes[1], mixes[2])
    fill(MIX_FIRST, None, mixes[0])
    fill(MIX_MID, None, mixes[1])


def by_columns(width, body):
    def step(n, carry):
        body(pl.ds(pl.multiple_of(n * COLS, COLS), COLS))
        return carry

    lax.fori_loop(0, width // COLS, step, 0)


def pack_kernel(take_ref, *refs):
    pieces, (out_ref, rows_ref, packed_ref, sem) = refs[:-4], refs[-4:]
    wide = packed_ref.shape[2]

    def leave(n):
        cols = pl.ds(pl.multiple_of(n * wide, wide), wide)
        return pltpu.make_async_copy(packed_ref.at[n], out_ref.at[:, cols], sem.at[n])

    def step(n, carry):
        cols = pl.ds(pl.multiple_of(n * wide, wide), wide)
        at = 0
        for piece in pieces:
            rows_ref[at : at + piece.shape[0], :] = piece[:, cols]
            at += piece.shape[0]
        packed_ref[n] = jnp.dot(
            take_ref[...], rows_ref[...], preferred_element_type=F32
        ).astype(BF16)
        leave(n).start()
        return carry

    parts = sem.shape[0]
    lax.fori_loop(0, parts, step, 0)
    for n in range(parts):
        leave(n).wait()


def expert_kernel(x, g0, g1, u0, u1, d0, d1, *refs):
    outs = refs[:-10]
    x_ref, grow_ref, down_ref, sum_ref, hidden_ref, y_ref, x_sem, grow_sem, down_sem, out_sem = (
        refs[-10:]
    )
    half = g0.shape[1]
    parts = x_sem.shape[0]
    deep = x.shape[1] // parts
    ends = out_sem.shape[0]
    wide = x.shape[1] // ends

    def row_copy(n):
        cols = pl.ds(pl.multiple_of(n * deep, deep), deep)
        return pltpu.make_async_copy(x.at[:, cols], x_ref.at[:, cols], x_sem.at[n])

    def grow_copies(slab, n, gate, up):
        rows = pl.ds(pl.multiple_of(n * deep, deep), deep)
        return [
            pltpu.make_async_copy(
                w.at[rows, :],
                grow_ref.at[slab, rows, pl.ds(at * half, half)],
                grow_sem.at[slab, n, at],
            )
            for at, w in enumerate((gate, up))
        ]

    def down_copies(n):
        cols = pl.ds(pl.multiple_of(n * wide, wide), wide)
        return [
            pltpu.make_async_copy(
                w.at[:, cols], down_ref.at[n, pl.ds(at * half, half), :], down_sem.at[n, at]
            )
            for at, w in enumerate((d0, d1))
        ]

    def leave(n):
        cols = pl.ds(pl.multiple_of(n * wide, wide), wide)
        copies, at = [], 0
        for c, out in enumerate(outs):
            rows = out.shape[1]
            copies.append(
                pltpu.make_async_copy(
                    y_ref.at[n, :, pl.ds(at, rows), :], out.at[:, :, cols], out_sem.at[n, c]
                )
            )
            at += rows
        return copies

    for slab, (gate, up) in enumerate(((g0, u0), (g1, u1))):
        for n in range(parts):
            if slab == 0:
                row_copy(n).start()
            for copy in grow_copies(slab, n, gate, up):
                copy.start()
    for n in range(ends):
        for copy in down_copies(n):
            copy.start()

    def grow(step, carry):
        slab, n = lax.div(step, parts), lax.rem(step, parts)

        @pl.when(slab == 0)
        def _():
            row_copy(n).wait()

        for copy in grow_copies(slab, n, g0, u0):
            copy.wait()
        part = pl.ds(pl.multiple_of(n * deep, deep), deep)
        grown = jnp.dot(x_ref[:, part], grow_ref[slab, part, :], preferred_element_type=F32)
        sum_ref[slab] += grown
        return carry

    sum_ref[...] = jnp.zeros(sum_ref.shape, F32)
    lax.fori_loop(0, 2 * parts, grow, 0)
    for slab in range(2):
        gate, up = sum_ref[slab, :, :half], sum_ref[slab, :, half:]
        hidden = gate / (1.0 + jnp.exp(-gate)) * up
        hidden_ref[:, slab * half : (slab + 1) * half] = hidden.astype(BF16)

    def shrink(n, carry):
        for copy in down_copies(n):
            copy.wait()
        y = jnp.dot(hidden_ref[...], down_ref[n], preferred_element_type=F32)
        y_ref[n] = y.reshape(y_ref.shape[1:]).astype(BF16)
        for copy in leave(n):
            copy.start()
        return carry

    lax.fori_loop(0, ends, shrink, 0)
    for n in range(ends):
        for copy in leave(n):
            copy.wait()


def weighted(mix_ref, first, last, y):
    return jnp.dot(mix_ref[0, first:last, :], y, preferred_element_type=F32) + jnp.dot(
        mix_ref[1, first:last, :], y, preferred_element_type=F32
    )


def far_kernel(mix_ref, y_ref, own_ref, third_ref, right_ref, left_ref):
    tok = own_ref.shape[0]
    half = tok // 2

    def body(cols):
        mixed = weighted(mix_ref, 0, mix_ref.shape[1], y_ref[:, cols])
        own_ref[:, cols] = mixed[:tok]
        third_ref[:, cols] = mixed[tok : 3 * tok]
        right_ref[:, cols] = mixed[3 * tok : 3 * tok + half].astype(BF16)
        left_ref[:, cols] = mixed[3 * tok + half :].astype(BF16)

    by_columns(y_ref.shape[1], body)


def third_kernel(third_ref, from_left_ref, from_right_ref, right_ref, left_ref):
    tok = right_ref.shape[0]
    half = tok // 2

    def body(cols):
        from_left = from_left_ref[:, cols].astype(F32)
        from_right = from_right_ref[:, cols].astype(F32)
        right_ref[:half, cols] = (third_ref[tok : tok + half, cols] + from_left).astype(BF16)
        right_ref[half:, cols] = third_ref[tok + half :, cols].astype(BF16)
        left_ref[:half, cols] = third_ref[:half, cols].astype(BF16)
        left_ref[half:, cols] = (third_ref[half:tok, cols] + from_right).astype(BF16)

    by_columns(right_ref.shape[1], body)


def second_kernel(
    mix, y_ref, from_left, from_right, right_ref, left_ref, mix_ref, from_left_ref, from_right_ref, sem
):
    tok = right_ref.shape[0]
    copies = [
        pltpu.make_async_copy(
            mix.at[n, pl.ds(2 * tok, 2 * tok), :], mix_ref.at[n], sem.at[n]
        )
        for n in range(2)
    ]
    copies.append(pltpu.make_async_copy(from_left, from_left_ref, sem.at[2]))
    copies.append(pltpu.make_async_copy(from_right, from_right_ref, sem.at[3]))
    for copy in copies:
        copy.start()
    for copy in copies[:2]:
        copy.wait()

    def body(cols):
        mixed = weighted(mix_ref, 0, 2 * tok, y_ref[:, cols])

        @pl.when(cols.start == 0)
        def _():
            for copy in copies[2:]:
                copy.wait()

        left_ref[:, cols] = (mixed[:tok] + from_right_ref[:, cols].astype(F32)).astype(BF16)
        right_ref[:, cols] = (mixed[tok:] + from_left_ref[:, cols].astype(F32)).astype(BF16)

    by_columns(y_ref.shape[1], body)


def first_kernel(
    near_ref, near_y_ref, mix_ref, y_ref, resid_ref, own_ref, base_ref, first_ref
):
    tok = resid_ref.shape[0]

    def body(cols):
        near = weighted(near_ref, 0, 3 * tok, near_y_ref[:, cols])
        mixed = weighted(mix_ref, 0, 2 * tok, y_ref[:, cols])
        base_ref[:, cols] = near[:tok] + own_ref[:, cols] + resid_ref[:, cols].astype(F32)
        first_ref[:, cols] = near[tok:] + mixed

    by_columns(y_ref.shape[1], body)


def add_kernel(first_ref, from_left_ref, from_right_ref, right_ref, left_ref):
    tok = right_ref.shape[0]
    left_ref[...] = (first_ref[:tok] + from_right_ref[...].astype(F32)).astype(BF16)
    right_ref[...] = (first_ref[tok:] + from_left_ref[...].astype(F32)).astype(BF16)


def last_kernel(base_ref, from_left_ref, from_right_ref, out_ref):
    total = base_ref[...] + from_left_ref[...].astype(F32) + from_right_ref[...].astype(F32)
    out_ref[...] = total.astype(BF16)


def ring(block, pools):
    right = [(k, (k + 1) % pools) for k in range(pools)]
    left = [(k, (k - 1) % pools) for k in range(pools)]
    pieces = [block]
    from_left = from_right = block
    for _ in range(1, pools // 2):
        from_left = lax.ppermute(from_left, "pool", right)
        from_right = lax.ppermute(from_right, "pool", left)
        pieces += [from_left, from_right]
    half = block.shape[0] // 2
    pieces += [
        lax.ppermute(from_left[:half], "pool", right),
        lax.ppermute(from_right[half:], "pool", left),
    ]
    return pieces


def shards(
    residual,
    queries,
    fresh_kv,
    pool_cache,
    hit_blocks,
    norm_gain,
    route_ids,
    route_logits,
    w_gate,
    w_up,
    w_down,
):
    pools = lax.axis_size("pool")
    plane = lax.axis_size("xy")
    rank = lax.axis_index("pool").astype(jnp.int32)[None]
    _, tok, model = queries.shape
    held, block, width = pool_cache.shape
    hits = hit_blocks.shape[1]
    top = route_ids.shape[2]
    half = w_gate.shape[2]
    shape = jax.ShapeDtypeStruct

    swap = [(0, 1), (1, 0)]
    own = (w_gate[0], w_up[0], w_down[0])
    peer = tuple(lax.ppermute(w, "core", swap) for w in own)

    (packed,) = held_call(
        gather_kernel,
        "gather_block",
        [shape((tok, 2 * width + META), BF16)],
        [
            rank,
            hit_blocks,
            (pool_cache,),
            Fetched((fresh_kv[0],)),
            Fetched((route_ids[0].T,)),
            Fetched((route_logits[0].T,)),
        ],
        scalars=2,
        near=(0,),
        scratch=[pltpu.SemaphoreType.DMA((HOT,))],
    )
    pieces = ring(packed, pools)

    stack = 4
    keys = hits * block + pools * tok
    attended, resid, normed, meta = held_call(
        lambda *refs: attend_kernel(*refs, pools=pools, held=held),
        "attend",
        [shape((tok, model), BF16)] * 3 + [shape((pools * tok, META), BF16)],
        [
            rank,
            hit_blocks,
            Fetched((norm_gain[None],)),
            Fetched((queries[0],)),
            Fetched((residual[0],)),
            *pieces,
        ],
        scalars=2,
        near=(2, 3),
        scratch=[
            pltpu.VMEM((pools * tok, 2 * width + META), BF16),
            pltpu.VMEM((keys, width), BF16),
            pltpu.VMEM((stack * tok, pools * tok), F32),
        ],
    )

    def size(table):
        return plane * len(table[0]), table[2] * tok

    mixing = (MIX_FIRST, MIX_MID, MIX_FAR)
    take_near, take_far, mix_first, mix_mid, mix_far = held_call(
        lambda *refs: route_kernel(*refs, pools=pools, top=top),
        "route",
        [shape(size(t), BF16) for t in (TAKE_NEAR, TAKE_FAR)]
        + [shape((2,) + size(t)[::-1], BF16) for t in mixing],
        [rank, meta],
        scalars=1,
        near=(0,),
        scratch=[pltpu.VMEM(size(TAKE_NEAR)[::-1], F32)],
    )

    def pack(take, parts_in, name):
        slots, rows = (take[0] if isinstance(take, tuple) else take).shape
        parts = model // COLS
        (out,) = held_call(
            pack_kernel,
            name,
            [shape((slots, model), BF16)],
            [take, *parts_in],
            far=(0,),
            scratch=[
                pltpu.VMEM((rows, COLS), BF16),
                pltpu.VMEM((parts, slots, COLS), BF16),
                pltpu.SemaphoreType.DMA((parts,)),
            ],
            limit=32,
        )
        return out

    def exchange(x):
        x = x.reshape(plane, -1, model)
        return lax.all_to_all(x, "xy", split_axis=0, concat_axis=0, tiled=True).reshape(
            -1, model
        )

    def expert(x, splits, name):
        slots = x.shape[0]
        parts, ends = 4, 4
        dma = pltpu.SemaphoreType.DMA
        return held_call(
            expert_kernel,
            name,
            [shape((plane, rows, model), BF16) for rows in splits],
            [(x,)] + [(w,) for pair in zip(own, peer) for w in pair],
            far=range(len(splits)),
            scratch=[
                pltpu.VMEM((slots, model), BF16),
                pltpu.VMEM((2, model, 2 * half), BF16),
                pltpu.VMEM((ends, 2 * half, model // ends), BF16),
                pltpu.VMEM((2, slots, 2 * half), F32),
                pltpu.VMEM((slots, 2 * half), BF16),
                pltpu.VMEM((ends, plane, slots // plane, model // ends), BF16),
                dma((parts,)),
                dma((2, parts, 2)),
                dma((ends, 2)),
                dma((ends, len(splits))),
            ],
            limit=48,
        )

    right = [(k, (k + 1) % pools) for k in range(pools)]
    left = [(k, (k - 1) % pools) for k in range(pools)]
    send = lambda r, l: (lax.ppermute(r, "pool", right), lax.ppermute(l, "pool", left))
    tie = lax.optimization_barrier

    once = send(normed, normed)
    once, take_near, peer = tie((once, take_near, peer))
    twice = send(*once)
    sent_near = pack(take_near, [normed, *once, *twice], "pack_near")
    thrice = send(*twice)
    fourth = send(thrice[0][: tok // 2], thrice[1][tok // 2 :])
    sent_far = pack(Fetched((take_far,)), [Fetched((normed,)), *thrice, *fourth], "pack_far")
    got_near = exchange(sent_near)
    got_near, sent_far = tie((got_near, sent_far))
    got_far = exchange(sent_far)
    out_first, out_mid = expert(got_near, (len(FIRST), len(MID)), "expert_near")
    got_far, out_first, out_mid = tie((got_far, out_first, out_mid))
    (out_far,) = expert(got_far, (len(FAR),), "expert_far")
    back_far = exchange(out_far)
    out_mid, back_far = tie((out_mid, back_far))
    back_mid = exchange(out_mid)
    out_first, back_mid = tie((out_first, back_mid))
    back_first = exchange(out_first)

    row, pair = (tok, model), (2 * tok, model)
    own_far, third, *moving = held_call(
        far_kernel,
        "mix_far",
        [shape(row, F32), shape(pair, F32)] + [shape((tok // 2, model), BF16)] * 2,
        [Fetched((mix_far,)), Fetched((back_far,))],
        near=(1, 2, 3),
    )
    moving = held_call(
        third_kernel,
        "add_third",
        [shape(row, BF16)] * 2,
        [third, *send(*moving)],
        near=(0, 1),
        limit=16,
    )
    moving = held_call(
        second_kernel,
        "mix_second",
        [shape(row, BF16)] * 2,
        [in_hbm(mix_mid), back_mid, *[in_hbm(m) for m in send(*moving)]],
        near=(0, 1),
        scratch=[
            pltpu.VMEM((2, 2 * tok, plane * len(MID)), BF16),
            pltpu.VMEM(row, BF16),
            pltpu.VMEM(row, BF16),
            pltpu.SemaphoreType.DMA((4,)),
        ],
        limit=24,
    )
    moving = send(*moving)
    base, first = held_call(
        first_kernel,
        "mix_first",
        [shape(row, F32), shape(pair, F32)],
        [
            Fetched((mix_first,)),
            Fetched((back_first,)),
            Fetched((mix_mid,)),
            back_mid,
            Fetched((resid,)),
            Fetched((own_far,)),
        ],
        near=(0, 1),
        limit=24,
    )
    moving = held_call(
        add_kernel, "add_first", [shape(row, BF16)] * 2, [first, *moving], near=(0, 1), limit=16
    )
    (layer_out,) = held_call(
        last_kernel, "add_last", [shape(row, BF16)], [base, *send(*moving)], limit=16
    )
    return (attended[None], layer_out[None])


def solution(mesh):
    pools, experts = mesh.devices.shape
    fine = Mesh(mesh.devices.reshape(pools, experts // 2, 2), ("pool", "xy", "core"))
    ex = ("xy", "core")
    tokens = P(ex, "pool", None)
    slab = P(("pool", "xy", "core"), None, None)
    placed = (
        tokens,
        tokens,
        tokens,
        P("pool", None, None),
        P(ex, None),
        P(),
        tokens,
        tokens,
        slab,
        slab,
        slab,
    )
    return jax.shard_map(
        shards, mesh=fine, in_specs=placed, out_specs=(tokens, tokens), check_vma=False
    )
```
